512 devices in a mesh: dp: 64 (over y, z), mp: 8 (over x, core).
Axes of the slice: x: 4, y: 4, z: 16, core: 2. Of those that a mesh axis runs over, the one named last changes fastest.
Arguments:
- x_in: bfloat16 [25600, 2048], P('dp'), may hold values from -6 to 6
- cotangent: bfloat16 [25600, 7168], P('dp', 'mp'), may hold values from -6 to 6
- w_gate: bfloat16 [2048, 7168], P('dp', 'mp'), may hold values from -0.125 to 0.125
- w_up: bfloat16 [2048, 7168], P('dp', 'mp'), may hold values from -0.125 to 0.125
- send_counts: int32 [64, 64], P('dp'), may hold values from 0 to 4, as said below
- recv_counts: int32 [64, 64], P('dp'), may hold values from 0 to 4, as said below
Outputs:
- grad_x: bfloat16 [25600, 2048], P('dp', 'mp')
- grad_gate: float32 [2048, 7168], P('dp', 'mp')
The draws below stay inside these ranges and needn't reach their ends.
Inputs may be any that keep to these rules, and one draw needn't show every extreme that they name: `send_counts`: each entry is 0 to 4. A quarter of the indices only send and the rest only receive; one sending index sends 4 rows to every receiver, so its live rows reach 400. recv_counts is the transpose of send_counts.
All inputs are finite; a program needn't handle non-finite values.
Results may differ from the reference program's by a relative error of at most 0.014.
Values may be sent and summed in bfloat16 or wider, within the bound.
A program may use at most 64 MiB of HBM per device.

```python
import jax
import jax.numpy as jnp
from jax import lax

D = 2048
FF = 7168
BAL = 208
SLOT = 4
CAP = 400
ROWS = 25600
N_DP = 64
N_MP = 8


def plan_counts(key):
    order = jax.random.permutation(jax.random.fold_in(key, 11), N_DP)
    heavy = order < N_DP // 4
    spread = jax.random.randint(jax.random.fold_in(key, 12), (N_DP, N_DP), 0, SLOT + 1)
    spread = jnp.where((order == 0)[:, None], SLOT, spread)
    pairs = heavy[:, None] & jnp.logical_not(heavy)[None, :]
    return jnp.where(pairs, spread, 0).astype(jnp.int32)


def draw_send_counts(key, part):
    return plan_counts(key)


def draw_recv_counts(key, part):
    return plan_counts(key).T


def steps_of(key, extent, cuts, low, high):
    def one(dim, blocks):
        heights = jax.random.uniform(jax.random.fold_in(jax.random.fold_in(key, 6), dim), (blocks,), jnp.float32, low / len(cuts), high / len(cuts))
        return jnp.repeat(jnp.exp(heights), extent[dim] // blocks).reshape((-1,) + (1,) * (len(extent) - dim - 1))

    gain = one(*cuts[0])
    for cut in cuts[1:]:
        gain = gain * one(*cut)
    return gain


def bell_draw(rng, dims, deviation, limit, split=(), kind=jnp.bfloat16):
    gain = steps_of(rng, dims, split, -0.22, 0.18) if split else 1.0
    result = jax.random.normal(rng, dims, jnp.float32) * deviation * gain
    return jnp.minimum(jnp.maximum(result, -limit), limit).astype(kind)


def setup_inputs(seed: int = 0) -> dict:
    streams_of = jax.random.split(jax.random.key(seed), 7)
    x_in = bell_draw(streams_of[0], (ROWS, D), 1.0, 6.0, ((0, 64),))
    cotangent = bell_draw(streams_of[1], (ROWS, FF), 1.0, 6.0, ((0, 64), (1, 8)))
    w_gate = bell_draw(streams_of[2], (D, FF), D ** -0.5, 0.125, ((0, 64), (1, 8)))
    w_up = bell_draw(streams_of[3], (D, FF), D ** -0.5, 0.125, ((0, 64), (1, 8)))
    send_counts = draw_send_counts(jax.random.fold_in(streams_of[6], 71), 0)
    recv_counts = draw_recv_counts(jax.random.fold_in(streams_of[6], 71), 0)
    return dict(x_in=x_in, cotangent=cotangent, w_gate=w_gate, w_up=w_up, send_counts=send_counts, recv_counts=recv_counts)


def reference(x_in, cotangent, w_gate, w_up, send_counts, recv_counts):
    sent_total = jnp.sum(send_counts, axis=1).astype(jnp.int32)
    got_total = jnp.sum(recv_counts, axis=1).astype(jnp.int32)
    live = (BAL + sent_total - got_total).astype(jnp.int32)
    live_end = jnp.cumsum(live).astype(jnp.int32)
    live_start = (live_end - live).astype(jnp.int32)
    position = jnp.arange(N_DP * BAL, dtype=jnp.int32)
    owner = jnp.sum((live_end[None, :] <= position[:, None]).astype(jnp.int32), axis=1).astype(jnp.int32)
    row_index = (owner * CAP + position - live_start[owner]).astype(jnp.int32)
    x_rows = x_in[row_index]
    cot_rows = cotangent[row_index]
    hidden_group = FF // N_MP
    gate_three = w_gate.astype(jnp.float32).reshape(D, N_MP, hidden_group)
    up_three = w_up.astype(jnp.float32).reshape(D, N_MP, hidden_group)

    def step(grad_total, block):
        x_block, cot_block = block
        gate_val = jnp.dot(x_block, w_gate, preferred_element_type=jnp.float32)
        up_val = jnp.dot(x_block, w_up, preferred_element_type=jnp.float32)
        sig = jax.nn.sigmoid(gate_val)
        cot_val = cot_block.astype(jnp.float32)
        d_gate = (cot_val * up_val * sig * (1.0 + gate_val * (1.0 - sig))).astype(jnp.bfloat16)
        d_up = (cot_val * gate_val * sig).astype(jnp.bfloat16)
        partial_value = jnp.einsum("rmf,dmf->rmd", d_gate.astype(jnp.float32).reshape(BAL, N_MP, hidden_group), gate_three)
        partial_value = partial_value + jnp.einsum("rmf,dmf->rmd", d_up.astype(jnp.float32).reshape(BAL, N_MP, hidden_group), up_three)
        rounded = lax.optimization_barrier(partial_value.astype(jnp.bfloat16))
        grad_rows = jnp.sum(rounded.astype(jnp.float32), axis=1).astype(jnp.bfloat16)
        grad_total = grad_total + lax.dot_general(x_block, d_gate, (((0,), (0,)), ((), ())), preferred_element_type=jnp.float32)
        return grad_total, grad_rows

    start = jnp.zeros((D, FF), jnp.float32)
    grad_gate, grad_rows = lax.scan(step, start, (x_rows.reshape(N_DP, BAL, D), cot_rows.reshape(N_DP, BAL, FF)))
    grad_x = jnp.zeros((N_DP * CAP, D), jnp.bfloat16).at[row_index].set(grad_rows.reshape(N_DP * BAL, D))
    return grad_x, grad_gate
```

```python
import jax
import jax.numpy as jnp
from jax import lax
from jax.sharding import PartitionSpec as P

BAL = 208


def contract_last(left, right):
    return lax.dot_general(
        left, right, (((1,), (1,)), ((), ())), preferred_element_type=jnp.float32
    )


def swiglu_back(x_rows, cot_rows, gate_full, up_full, live_mask):
    gate_val = jnp.dot(x_rows, gate_full, preferred_element_type=jnp.float32)
    up_val = jnp.dot(x_rows, up_full, preferred_element_type=jnp.float32)
    sig = jax.nn.sigmoid(gate_val)
    cot_val = cot_rows.astype(jnp.float32)
    d_gate = jnp.where(
        live_mask[:, None], cot_val * up_val * sig * (1.0 + gate_val * (1.0 - sig)), 0.0
    ).astype(jnp.bfloat16)
    d_up = jnp.where(live_mask[:, None], cot_val * gate_val * sig, 0.0).astype(jnp.bfloat16)
    partial_value = contract_last(d_gate, gate_full) + contract_last(d_up, up_full)
    return (partial_value, d_gate)


def group_sum(partial_value):
    return lax.psum_scatter(
        partial_value.astype(jnp.bfloat16), "mp", scatter_dimension=1, tiled=True
    )


def on_device(x_in, cotangent, w_gate, w_up, send_counts, recv_counts):
    rows_cap = x_in.shape[0]
    width = x_in.shape[1]
    dev_count = lax.axis_size("dp")
    gate_full, up_full = (
        lax.all_gather(w_gate, "dp", axis=0, tiled=True),
        lax.all_gather(w_up, "dp", axis=0, tiled=True),
    )
    sent = send_counts[0]
    got = recv_counts[0]
    live_rows = BAL + jnp.sum(sent) - jnp.sum(got)
    live_mask = jnp.arange(rows_cap) < live_rows
    partial_value, d_gate = swiglu_back(x_in, cotangent, gate_full, up_full, live_mask)
    grad_x = group_sum(partial_value)
    block_rows = width // dev_count
    whole = lax.dot_general(
        x_in, d_gate, (((0,), (0,)), ((), ())), preferred_element_type=jnp.float32
    )
    grad_gate = lax.psum_scatter(whole.astype(jnp.bfloat16), "dp", scatter_dimension=0, tiled=True).astype(jnp.float32)
    return (grad_x, grad_gate)


def solution(mesh):
    return jax.shard_map(
        on_device,
        mesh=mesh,
        in_specs=(
            P("dp", None),
            P("dp", "mp"),
            P("dp", "mp"),
            P("dp", "mp"),
            P("dp", None),
            P("dp", None),
        ),
        out_specs=(P("dp", "mp"), P("dp", "mp")),
        check_vma=False,
    )
```

```python
import functools

import jax
import jax.numpy as jnp
from jax import lax
from jax.experimental import pallas as pl
from jax.experimental.pallas import tpu as pltpu
from jax.sharding import PartitionSpec as P

BAL = 208
RING_Y = 4
MESH = pl.DeviceIdType.MESH
VMEM = pl.BlockSpec(memory_space=pltpu.VMEM)


def place(nz):
    me = lax.axis_index("dp")
    y, z = lax.div(me, nz), lax.rem(me, nz)

    def index(yo, zo):
        return lax.rem(y + yo + 2 * RING_Y, RING_Y) * nz + lax.rem(z + zo + 2 * nz, nz)

    return index


def greet(index):
    barrier = pltpu.get_barrier_semaphore()
    for yo, zo in ((0, 1), (0, -1), (1, 0), (-1, 0)):
        pl.semaphore_signal(
            barrier, inc=1, device_id={"dp": index(yo, zo)}, device_id_type=MESH
        )
    pl.semaphore_wait(barrier, 4)


def reach(nz, stream, way):
    forward = stream in ("a", 0)
    return nz // 2 if forward == (way == 0) else nz // 2 - 1


def gather_kernel(
    nz, cut, half_a, half_b, w_ref, out_ref, za_s, za_r, zb_s, zb_r, ya_s, ya_r, yb_s, yb_r, own
):
    index = place(nz)
    rows, cols = w_ref.shape
    top = nz // 2
    spans = {"a": (0, cut), "b": (cut, cols - cut)}
    halves = {
        "a": ((0, half_a), (half_a, cut - half_a)),
        "b": ((cut, half_b), (cut + half_b, cols - cut - half_b)),
    }

    def block(yo, zo, span):
        start = pl.multiple_of(index(yo, zo) * rows, rows)
        return out_ref.at[pl.ds(start, rows), pl.ds(span[0], span[1])]

    def copy(src, dst, target, s_sem, r_sem):
        return pltpu.make_async_remote_copy(
            src_ref=src, dst_ref=dst, send_sem=s_sem, recv_sem=r_sem,
            device_id={"dp": index(*target)}, device_id_type=MESH,
        )

    def origin(way, k):
        return -k if way == 0 else k

    def onward(way):
        return (0, 1) if way == 0 else (0, -1)

    def z_copy(stream, way, k, mine=False):
        span = spans["a"] if stream == "a" else spans["b"]
        yo = 0 if stream == "a" else stream
        dst = block(yo, origin(way, k - 1), span)
        src = w_ref.at[:, pl.ds(span[0], span[1])] if mine else dst
        sems = (za_s.at[way, k], za_r.at[way, k]) if stream == "a" else (
            zb_s.at[way, k, stream], zb_r.at[way, k, stream])
        return copy(src, dst, onward(way), *sems)

    def z_wait(stream, way, k):
        span = spans["a"] if stream == "a" else spans["b"]
        yo = 0 if stream == "a" else stream
        dst = block(yo, origin(way, k), span)
        sem = za_r.at[way, k] if stream == "a" else zb_r.at[way, k, stream]
        other = za_s.at[way, k] if stream == "a" else zb_s.at[way, k, stream]
        copy(dst, dst, onward(way), other, sem).wait_recv()

    def y_sems(kind, c, part):
        if kind == "a":
            return ya_s.at[c, part], ya_r.at[c, part]
        return yb_s.at[part], yb_r.at[part]

    def y_part(kind, part):
        return spans[kind] if part < 2 else halves[kind][part - 2]

    def y_copy(kind, zo, c, part, mine=False):
        span = y_part(kind, part)
        yo = 0 if part < 2 else (-1 if part == 2 else 1)
        dst = block(yo, zo, span)
        src = w_ref.at[:, pl.ds(span[0], span[1])] if mine else dst
        return copy(src, dst, (1, 0) if part % 2 == 0 else (-1, 0), *y_sems(kind, c, part))

    def y_wait(kind, zo, c, part):
        yo = (-1, 1, -2, 2)[part]
        dst = block(yo, zo, y_part(kind, part))
        copy(dst, dst, (1, 0), *y_sems(kind, c, part)).wait_recv()

    def cell(way, k):
        return 2 * k - 1 + way

    def y_pass(kind, zo, c):
        for part in (0, 1):
            y_wait(kind, zo, c, part)
            y_copy(kind, zo, c, part + 2).start()

    greet(index)
    keep = pltpu.make_async_copy(w_ref, out_ref.at[pl.ds(pl.multiple_of(index(0, 0) * rows, rows), rows), :], own)
    keep.start()
    for part in (0, 1):
        y_copy("b", 0, 0, part, True).start()
    for way in (0, 1):
        z_copy("a", way, 1, True).start()
        z_copy(0, way, 1, True).start()
    for part in (0, 1):
        y_copy("a", 0, 0, part, True).start()
    for part in (0, 1):
        y_wait("b", 0, 0, part)
        y_copy("b", 0, 0, part + 2).start()
        for way in (0, 1):
            z_copy(3 if part == 0 else 1, way, 1).start()

    def step(k, known, first=False):
        def arrives(stream, way):
            return not known or k <= reach(nz, stream, way)

        def goes_on(stream, way):
            return not known or k + 1 <= reach(nz, stream, way)

        for way in (0, 1):
            if arrives("a", way):
                z_wait("a", way, k)
                if goes_on("a", way):
                    z_copy("a", way, k + 1).start()
                for part in (0, 1):
                    y_copy("a", origin(way, k), cell(way, k), part).start()
        if first:
            for part in (2, 3):
                y_wait("b", 0, 0, part)
            for way in (0, 1):
                z_copy(2, way, 1).start()
        for stream in (0, 3, 1, 2):
            for way in (0, 1):
                if arrives(stream, way):
                    z_wait(stream, way, k)
                    if goes_on(stream, way):
                        z_copy(stream, way, k + 1).start()
        if first:
            y_pass("a", 0, 0)
        else:
            for way in (0, 1):
                y_pass("a", origin(way, k - 1), cell(way, k - 1))

    step(1, True, True)
    if top > 3:
        def body(k, carry):
            step(k, False)
            return carry

        lax.fori_loop(2, top - 1, body, 0)
    if top > 2:
        step(top - 1, True)
    step(top, True)
    y_pass("a", -top, cell(0, top))

    def drain_y(c, zo):
        for part in (2, 3):
            y_wait("a", zo, c, part)
        for part in range(4):
            y_copy("a", zo, c, part).wait_send()

    drain_y(0, 0)
    for part in range(4):
        y_copy("b", 0, 0, part).wait_send()

    def drain(k, known):
        for way in (0, 1):
            for stream in ("a", 0, 1, 2, 3):
                if not known or k <= reach(nz, stream, way):
                    z_copy(stream, way, k).wait_send()
            if not known or k <= reach(nz, "a", way):
                drain_y(cell(way, k), origin(way, k))

    def drain_body(k, carry):
        drain(k, False)
        return carry

    lax.fori_loop(1, top, drain_body, 0)
    drain(top, True)
    keep.wait()


def gather_rows(shard, ranks):
    rows, cols = shard.shape
    nz = ranks // RING_Y
    tiles = cols // 128
    cut = 128 * max(2, round(tiles * 0.633))
    half_a = 128 * ((cut // 128 + 1) // 2)
    half_b = 128 * (((cols - cut) // 128 + 1) // 2)
    dma = pltpu.SemaphoreType.DMA
    k = nz // 2 + 1
    return pl.pallas_call(
        functools.partial(gather_kernel, nz, cut, half_a, half_b),
        out_shape=jax.ShapeDtypeStruct((ranks * rows, cols), shard.dtype),
        in_specs=[VMEM],
        out_specs=pl.BlockSpec(memory_space=pl.ANY),
        scratch_shapes=[
            dma((2, k)), dma((2, k)), dma((2, k, 4)), dma((2, k, 4)),
            dma((nz, 4)), dma((nz, 4)), dma((4,)), dma((4,)), dma,
        ],
        compiler_params=pltpu.CompilerParams(collective_id=0, has_side_effects=True),
        name="gather_rows",
    )(shard)


def scatter_kernel(
    nz, cut, half_a, half_b, p_ref, out_ref,
    far, near, near_out, za_in, za_out, zb_in, zb_out, b_sum, b_far, b_near, b_near_out,
    far_s, far_r, near_s, near_r, za_s, za_r, zb_s, zb_r, bf_s, bf_r, bn_s, bn_r,
):
    index = place(nz)
    rows, cols = out_ref.shape
    top = nz // 2
    f32, bf16 = jnp.float32, jnp.bfloat16
    wide_b = cols - cut
    halves_a = ((0, half_a), (half_a, cut - half_a))
    halves_b = ((0, half_b), (half_b, wide_b - half_b))

    def mine(yo, zo, start, size):
        row = pl.multiple_of(index(yo, zo) * rows, rows)
        return p_ref.at[pl.ds(row, rows), pl.ds(start, size)]

    def copy(src, dst, target, s_sem, r_sem):
        return pltpu.make_async_remote_copy(
            src_ref=src, dst_ref=dst, send_sem=s_sem, recv_sem=r_sem,
            device_id={"dp": index(*target)}, device_id_type=MESH,
        )

    side = ((1, 0), (-1, 0))
    onward = ((0, 1), (0, -1))

    def toward(way, m):
        return m if way == 0 else -m

    def cell(way, m):
        return 2 * m - 1 + way

    def far_copy(zo, c, part):
        start, size = halves_a[part]
        return copy(mine(2, zo, start, size), far.at[c, :, pl.ds(start, size)], side[part],
                    far_s.at[c, part], far_r.at[c, part])

    def near_copy(c, part):
        return copy(near_out.at[c, part], near.at[c, part], side[part],
                    near_s.at[c, part], near_r.at[c, part])

    def stage_1(zo, c):
        for part in (0, 1):
            far_copy(zo, c, part).start()

    def stage_2(zo, c):
        for part in (0, 1):
            start, size = halves_a[part]
            rest, rest_size = halves_a[1 - part]
            yo = 1 if part == 0 else -1
            near_out[c, part, :, pl.ds(rest, rest_size)] = mine(yo, zo, rest, rest_size)[...]
            far_copy(zo, c, part).wait_recv()
            total = mine(yo, zo, start, size)[...].astype(f32) + far[c, :, pl.ds(start, size)].astype(f32)
            near_out[c, part, :, pl.ds(start, size)] = total.astype(bf16)
            near_copy(c, part).start()

    def stage_3(zo, c):
        for part in (0, 1):
            near_copy(c, part).wait_recv()
        return (mine(0, zo, 0, cut)[...].astype(f32) + near[c, 0].astype(f32)) + near[c, 1].astype(f32)

    def za_copy(way, m):
        return copy(za_out.at[way, m], za_in.at[way, m], onward[way], za_s.at[way, m], za_r.at[way, m])

    def zb_copy(way, m, stream, src=None):
        return copy(zb_out.at[way, m, stream] if src is None else src, zb_in.at[way, m, stream],
                    onward[way], zb_s.at[way, m, stream], zb_r.at[way, m, stream])

    def cells(m, known):
        if known and m == 0:
            return ((0, 0),)
        return tuple((toward(way, m), cell(way, m)) for way in (0, 1)
                     if not known or m <= reach(nz, "a", way))

    def ahead(m, known, stage):
        for zo, c in cells(m, known):
            stage(zo, c)

    def z_step(m, known):
        for stream in (0, 1, 2, 3):
            for way in (0, 1):
                limit = reach(nz, stream, way)
                if known and m > limit:
                    continue
                block = mine(stream, toward(way, m), cut, wide_b)
                if known and m == limit:
                    zb_copy(way, m - 1, stream, block).start()
                else:
                    zb_copy(way, m, stream).wait_recv()
                    total = block[...].astype(f32) + zb_in[way, m, stream].astype(f32)
                    zb_out[way, m - 1, stream] = total.astype(bf16)
                    zb_copy(way, m - 1, stream).start()
        for way in (0, 1):
            limit = reach(nz, "a", way)
            if known and m > limit:
                continue
            total = stage_3(toward(way, m), cell(way, m))
            if not (known and m == limit):
                za_copy(way, m).wait_recv()
                total = total + za_in[way, m].astype(f32)
            za_out[way, m - 1] = total.astype(bf16)
            za_copy(way, m - 1).start()

    greet(index)
    ahead(top, True, stage_1)
    ahead(top - 1, True, stage_1)
    ahead(top - 2, True, stage_1)
    ahead(top, True, stage_2)
    ahead(top - 1, True, stage_2)

    def iterate(m, known):
        if not known or m >= 3:
            ahead(m - 3, known, stage_1)
        if not known or m >= 2:
            ahead(m - 2, known, stage_2)
        z_step(m, known)

    peeled = [m for m in range(top, 0, -1) if m >= top - 1 or m <= 3]
    for m in [m for m in peeled if m >= top - 1]:
        iterate(m, True)
    inner = (top - 2) - 4 + 1
    if inner > 0:
        def body(i, carry):
            iterate(top - 2 - i, False)
            return carry

        lax.fori_loop(0, inner, body, 0)
    for m in [m for m in peeled if m < top - 1]:
        iterate(m, True)

    def b_final(stream):
        total = mine(stream, 0, cut, wide_b)[...].astype(f32)
        for way in (0, 1):
            zb_copy(way, 0, stream).wait_recv()
            total = total + zb_in[way, 0, stream].astype(f32)
        return total

    def bf_copy(part):
        start, size = halves_b[part]
        return copy(b_sum.at[:, pl.ds(start, size)], b_far.at[:, pl.ds(start, size)], side[part],
                    bf_s.at[part], bf_r.at[part])

    def bn_copy(part):
        return copy(b_near_out.at[part], b_near.at[part], side[part], bn_s.at[part], bn_r.at[part])

    b_sum[...] = b_final(2).astype(bf16)
    for part in (0, 1):
        bf_copy(part).start()
    next_to = (b_final(1), b_final(3))
    own_b = b_final(0)
    for part in (0, 1):
        start, size = halves_b[part]
        rest, rest_size = halves_b[1 - part]
        bf_copy(part).wait_recv()
        total = next_to[part]
        b_near_out[part, :, pl.ds(rest, rest_size)] = total[:, rest:rest + rest_size].astype(bf16)
        b_near_out[part, :, pl.ds(start, size)] = (
            total[:, start:start + size] + b_far[:, pl.ds(start, size)].astype(f32)).astype(bf16)
        bn_copy(part).start()
    total = stage_3(0, 0)
    for way in (0, 1):
        za_copy(way, 0).wait_recv()
        total = total + za_in[way, 0].astype(f32)
    out_ref[:, pl.ds(0, cut)] = total
    for part in (0, 1):
        bn_copy(part).wait_recv()
    out_ref[:, pl.ds(cut, wide_b)] = (own_b + b_near[0].astype(f32)) + b_near[1].astype(f32)

    def drain_y(zo, c):
        for part in (0, 1):
            far_copy(zo, c, part).wait_send()
            near_copy(c, part).wait_send()

    def drain(m, known):
        ahead(m, known, drain_y)
        for way in (0, 1):
            for stream in (0, 1, 2, 3):
                if not known or m <= reach(nz, stream, way):
                    zb_copy(way, m - 1, stream).wait_send()
            if not known or m <= reach(nz, "a", way):
                za_copy(way, m - 1).wait_send()

    drain_y(0, 0)

    def drain_body(m, carry):
        drain(m, False)
        return carry

    lax.fori_loop(1, top, drain_body, 0)
    drain(top, True)
    for part in (0, 1):
        bf_copy(part).wait_send()
        bn_copy(part).wait_send()


def scatter_sum(whole, ranks):
    rows, cols = whole.shape[0] // ranks, whole.shape[1]
    nz = ranks // RING_Y
    tiles = cols // 128
    cut = 128 * max(2, round(tiles * 0.633 + 0.2))
    half_a = 128 * ((cut // 128 + 1) // 2)
    wide_b = cols - cut
    half_b = 128 * ((wide_b // 128 + 1) // 2)
    k = nz // 2 + 1
    bf16 = jnp.bfloat16
    dma = pltpu.SemaphoreType.DMA
    return pl.pallas_call(
        functools.partial(scatter_kernel, nz, cut, half_a, half_b),
        out_shape=jax.ShapeDtypeStruct((rows, cols), jnp.float32),
        in_specs=[VMEM],
        out_specs=VMEM,
        scratch_shapes=[
            pltpu.VMEM((nz, rows, cut), bf16),
            pltpu.VMEM((nz, 2, rows, cut), bf16),
            pltpu.VMEM((nz, 2, rows, cut), bf16),
            pltpu.VMEM((2, k, rows, cut), bf16),
            pltpu.VMEM((2, k, rows, cut), bf16),
            pltpu.VMEM((2, k, 4, rows, wide_b), bf16),
            pltpu.VMEM((2, k, 4, rows, wide_b), bf16),
            pltpu.VMEM((rows, wide_b), bf16),
            pltpu.VMEM((rows, wide_b), bf16),
            pltpu.VMEM((2, rows, wide_b), bf16),
            pltpu.VMEM((2, rows, wide_b), bf16),
            dma((nz, 2)), dma((nz, 2)), dma((nz, 2)), dma((nz, 2)),
            dma((2, k)), dma((2, k)), dma((2, k, 4)), dma((2, k, 4)),
            dma((2,)), dma((2,)), dma((2,)), dma((2,)),
        ],
        compiler_params=pltpu.CompilerParams(
            collective_id=1, has_side_effects=True, vmem_limit_bytes=48 * 1024 * 1024),
        name="scatter_sum",
    )(whole)


def on_device(x_in, cotangent, w_gate, w_up, send_counts, recv_counts):
    ranks = lax.axis_size("dp")
    hidden = w_gate.shape[1]
    weights = gather_rows(jnp.concatenate([w_gate, w_up], axis=1), ranks)
    live_rows = BAL + jnp.sum(send_counts[0]) - jnp.sum(recv_counts[0])
    live = (jnp.arange(x_in.shape[0]) < live_rows)[:, None]
    both = jnp.dot(x_in, weights, preferred_element_type=jnp.float32)
    gate_val, up_val = both[:, :hidden], both[:, hidden:]
    sig = jax.nn.sigmoid(gate_val)
    cot_val = cotangent.astype(jnp.float32)
    d_gate = jnp.where(
        live, cot_val * up_val * sig * (1.0 + gate_val * (1.0 - sig)), 0.0
    ).astype(jnp.bfloat16)
    d_up = jnp.where(live, cot_val * gate_val * sig, 0.0).astype(jnp.bfloat16)
    whole = lax.dot_general(
        x_in, d_gate, (((0,), (0,)), ((), ())), preferred_element_type=jnp.float32
    ).astype(jnp.bfloat16)
    partial_value = lax.dot_general(
        jnp.concatenate([d_gate, d_up], axis=1), weights, (((1,), (1,)), ((), ())),
        preferred_element_type=jnp.float32,
    ).astype(jnp.bfloat16)
    partial_value, whole = lax.optimization_barrier((partial_value, whole))
    grad_x = lax.psum_scatter(partial_value, "mp", scatter_dimension=1, tiled=True)
    grad_gate = scatter_sum(whole, ranks)
    return (grad_x, grad_gate)


def solution(mesh):
    return jax.shard_map(
        on_device,
        mesh=mesh,
        in_specs=(
            P("dp", None),
            P("dp", "mp"),
            P("dp", "mp"),
            P("dp", "mp"),
            P("dp", None),
            P("dp", None),
        ),
        out_specs=(P("dp", "mp"), P("dp", "mp")),
        check_vma=False,
    )
```

```python
import functools

import jax
import jax.numpy as jnp
from jax import lax
from jax.experimental import pallas as pl
from jax.experimental.pallas import tpu as pltpu
from jax.sharding import PartitionSpec as P

BAL = 208
RING_Y = 4
MESH = pl.DeviceIdType.MESH
VMEM = pl.BlockSpec(memory_space=pltpu.VMEM)


def place(nz):
    me = lax.axis_index("dp")
    y, z = lax.div(me, nz), lax.rem(me, nz)

    def index(yo, zo):
        return lax.rem(y + yo + 2 * RING_Y, RING_Y) * nz + lax.rem(z + zo + 2 * nz, nz)

    return index


def greet(index, peers=()):
    barrier = pltpu.get_barrier_semaphore()
    for peer in peers:
        pl.semaphore_signal(barrier, inc=1, device_id={"mp": peer}, device_id_type=MESH)
    for yo, zo in ((0, 1), (0, -1), (1, 0), (-1, 0)):
        pl.semaphore_signal(
            barrier, inc=1, device_id={"dp": index(yo, zo)}, device_id_type=MESH
        )
    pl.semaphore_wait(barrier, 4 + len(peers))


def reach(nz, stream, way):
    forward = stream in ("a", 0)
    return nz // 2 if forward == (way == 0) else nz // 2 - 1


def gather_kernel(
    nz, cut, half_a, half_b, gate_ref, up_ref, sent_ref, got_ref, out_ref, live_ref,
    w_ref, za_s, za_r, zb_s, zb_r, ya_s, ya_r, yb_s, yb_r, own
):
    index = place(nz)
    rows, cols = w_ref.shape
    top = nz // 2
    spans = {"a": (0, cut), "b": (cut, cols - cut)}
    halves = {
        "a": ((0, half_a), (half_a, cut - half_a)),
        "b": ((cut, half_b), (cut + half_b, cols - cut - half_b)),
    }

    def block(yo, zo, span):
        start = pl.multiple_of(index(yo, zo) * rows, rows)
        return out_ref.at[pl.ds(start, rows), pl.ds(span[0], span[1])]

    def copy(src, dst, target, s_sem, r_sem):
        return pltpu.make_async_remote_copy(
            src_ref=src, dst_ref=dst, send_sem=s_sem, recv_sem=r_sem,
            device_id={"dp": index(*target)}, device_id_type=MESH,
        )

    def origin(way, k):
        return -k if way == 0 else k

    def onward(way):
        return (0, 1) if way == 0 else (0, -1)

    def z_copy(stream, way, k, mine=False):
        span = spans["a"] if stream == "a" else spans["b"]
        yo = 0 if stream == "a" else stream
        dst = block(yo, origin(way, k - 1), span)
        src = w_ref.at[:, pl.ds(span[0], span[1])] if mine else dst
        sems = (za_s.at[way, k], za_r.at[way, k]) if stream == "a" else (
            zb_s.at[way, k, stream], zb_r.at[way, k, stream])
        return copy(src, dst, onward(way), *sems)

    def z_wait(stream, way, k):
        span = spans["a"] if stream == "a" else spans["b"]
        yo = 0 if stream == "a" else stream
        dst = block(yo, origin(way, k), span)
        sem = za_r.at[way, k] if stream == "a" else zb_r.at[way, k, stream]
        other = za_s.at[way, k] if stream == "a" else zb_s.at[way, k, stream]
        copy(dst, dst, onward(way), other, sem).wait_recv()

    def y_sems(kind, c, part):
        if kind == "a":
            return ya_s.at[c, part], ya_r.at[c, part]
        return yb_s.at[part], yb_r.at[part]

    def y_part(kind, part):
        return spans[kind] if part < 2 else halves[kind][part - 2]

    def y_copy(kind, zo, c, part, mine=False):
        span = y_part(kind, part)
        yo = 0 if part < 2 else (-1 if part == 2 else 1)
        dst = block(yo, zo, span)
        src = w_ref.at[:, pl.ds(span[0], span[1])] if mine else dst
        return copy(src, dst, (1, 0) if part % 2 == 0 else (-1, 0), *y_sems(kind, c, part))

    def y_wait(kind, zo, c, part):
        yo = (-1, 1, -2, 2)[part]
        dst = block(yo, zo, y_part(kind, part))
        copy(dst, dst, (1, 0), *y_sems(kind, c, part)).wait_recv()

    def cell(way, k):
        return 2 * k - 1 + way

    def y_pass(kind, zo, c):
        for part in (0, 1):
            y_wait(kind, zo, c, part)
            y_copy(kind, zo, c, part + 2).start()

    hidden = gate_ref.shape[1]
    w_ref[:, pl.ds(0, hidden)] = gate_ref[...]
    w_ref[:, pl.ds(hidden, hidden)] = up_ref[...]
    change = jnp.sum((sent_ref[...] - got_ref[...]).astype(jnp.float32), axis=1, keepdims=True)
    live_ref[...] = jnp.broadcast_to(change + BAL, live_ref.shape)
    greet(index)
    keep = pltpu.make_async_copy(w_ref, out_ref.at[pl.ds(pl.multiple_of(index(0, 0) * rows, rows), rows), :], own)
    keep.start()
    for part in (0, 1):
        y_copy("b", 0, 0, part, True).start()
    for way in (0, 1):
        z_copy("a", way, 1, True).start()
    for part in (0, 1):
        y_copy("a", 0, 0, part, True).start()
    for way in (0, 1):
        z_copy(0, way, 1, True).start()

    def move(stream, way, k, known):
        if known and k > reach(nz, stream, way):
            return False
        z_wait(stream, way, k)
        if not known or k + 1 <= reach(nz, stream, way):
            z_copy(stream, way, k + 1).start()
        return True

    def a_step(k, known):
        for way in (0, 1):
            if move("a", way, k, known):
                for part in (0, 1):
                    y_copy("a", origin(way, k), cell(way, k), part).start()

    def a_pass(k, known):
        for way in (0, 1):
            if not known or k <= reach(nz, "a", way):
                y_pass("a", origin(way, k), cell(way, k))

    def b_step(k, known):
        for stream in (0, 3, 1, 2):
            for way in (0, 1):
                move(stream, way, k, known)

    a_step(1, True)
    for part in (0, 1):
        y_wait("b", 0, 0, part)
        y_copy("b", 0, 0, part + 2).start()
        for way in (0, 1):
            z_copy(3 if part == 0 else 1, way, 1).start()
    y_pass("a", 0, 0)
    a_step(2, top > 2 and 2 >= top - 1 or top == 2)
    for part in (2, 3):
        y_wait("b", 0, 0, part)
    for way in (0, 1):
        z_copy(2, way, 1).start()
    a_pass(1, True)

    def body(k, carry):
        a_step(k, False)
        b_step(k - 2, False)
        a_pass(k - 1, False)
        return carry

    if top > 4:
        lax.fori_loop(3, top - 1, body, 0)
    for k in range(max(3, top - 1), top + 1):
        a_step(k, True)
        b_step(k - 2, True)
        a_pass(k - 1, True)
    a_pass(top, True)
    b_step(top - 1, True)
    b_step(top, True)

    def drain_y(c, zo):
        for part in (2, 3):
            y_wait("a", zo, c, part)
        for part in range(4):
            y_copy("a", zo, c, part).wait_send()

    drain_y(0, 0)
    for part in range(4):
        y_copy("b", 0, 0, part).wait_send()

    def drain(k, known):
        for way in (0, 1):
            for stream in ("a", 0, 1, 2, 3):
                if not known or k <= reach(nz, stream, way):
                    z_copy(stream, way, k).wait_send()
            if not known or k <= reach(nz, "a", way):
                drain_y(cell(way, k), origin(way, k))

    def drain_body(k, carry):
        drain(k, False)
        return carry

    lax.fori_loop(1, top, drain_body, 0)
    drain(top, True)
    keep.wait()


def gather_rows(w_gate, w_up, sent, got, ranks):
    rows, cols = w_gate.shape[0], 2 * w_gate.shape[1]
    nz = ranks // RING_Y
    tiles = cols // 128
    cut = 128 * max(2, round(tiles * 0.633))
    half_a = 128 * ((cut // 128 + 1) // 2)
    half_b = 128 * (((cols - cut) // 128 + 1) // 2)
    dma = pltpu.SemaphoreType.DMA
    k = nz // 2 + 1
    return pl.pallas_call(
        functools.partial(gather_kernel, nz, cut, half_a, half_b),
        out_shape=(
            jax.ShapeDtypeStruct((ranks * rows, cols), w_gate.dtype),
            jax.ShapeDtypeStruct((8, 128), jnp.float32),
        ),
        in_specs=[VMEM] * 4,
        out_specs=(pl.BlockSpec(memory_space=pl.ANY), VMEM),
        scratch_shapes=[
            pltpu.VMEM((rows, cols), w_gate.dtype),
            dma((2, k)), dma((2, k)), dma((2, k, 4)), dma((2, k, 4)),
            dma((nz, 4)), dma((nz, 4)), dma((4,)), dma((4,)), dma,
        ],
        compiler_params=pltpu.CompilerParams(collective_id=0, has_side_effects=True),
        name="gather_rows",
    )(w_gate, w_up, sent, got)


def scatter_kernel(
    nz, peers, cut, half_a, half_b, p_ref, d_ref, weights_ref, out_ref, grad_x_ref, part_out, part_in,
    far, near, near_out, za_in, za_out, zb_in, zb_out, b_sum, b_far, b_near, b_near_out,
    part_s, part_r, far_s, far_r, near_s, near_r, za_s, za_r, zb_s, zb_r, bf_s, bf_r, bn_s, bn_r,
):
    index = place(nz)
    rows, cols = out_ref.shape
    top = nz // 2
    f32, bf16 = jnp.float32, jnp.bfloat16
    wide_b = cols - cut
    halves_a = ((0, half_a), (half_a, cut - half_a))
    halves_b = ((0, half_b), (half_b, wide_b - half_b))

    def mine(yo, zo, start, size):
        row = pl.multiple_of(index(yo, zo) * rows, rows)
        return p_ref.at[pl.ds(row, rows), pl.ds(start, size)]

    def copy(src, dst, target, s_sem, r_sem):
        return pltpu.make_async_remote_copy(
            src_ref=src, dst_ref=dst, send_sem=s_sem, recv_sem=r_sem,
            device_id={"dp": index(*target)}, device_id_type=MESH,
        )

    side = ((1, 0), (-1, 0))
    onward = ((0, 1), (0, -1))

    def toward(way, m):
        return m if way == 0 else -m

    def cell(way, m):
        return 2 * m - 1 + way

    def far_copy(zo, c, part):
        start, size = halves_a[part]
        return copy(mine(2, zo, start, size), far.at[c, :, pl.ds(start, size)], side[part],
                    far_s.at[c, part], far_r.at[c, part])

    def near_copy(c, part):
        return copy(near_out.at[c, part], near.at[c, part], side[part],
                    near_s.at[c, part], near_r.at[c, part])

    def stage_1(zo, c):
        for part in (0, 1):
            far_copy(zo, c, part).start()

    def stage_2(zo, c):
        for part in (0, 1):
            start, size = halves_a[part]
            rest, rest_size = halves_a[1 - part]
            yo = 1 if part == 0 else -1
            near_out[c, part, :, pl.ds(rest, rest_size)] = mine(yo, zo, rest, rest_size)[...]
            far_copy(zo, c, part).wait_recv()
            total = mine(yo, zo, start, size)[...].astype(f32) + far[c, :, pl.ds(start, size)].astype(f32)
            near_out[c, part, :, pl.ds(start, size)] = total.astype(bf16)
            near_copy(c, part).start()

    def stage_3(zo, c):
        for part in (0, 1):
            near_copy(c, part).wait_recv()
        return (mine(0, zo, 0, cut)[...].astype(f32) + near[c, 0].astype(f32)) + near[c, 1].astype(f32)

    def za_copy(way, m):
        return copy(za_out.at[way, m], za_in.at[way, m], onward[way], za_s.at[way, m], za_r.at[way, m])

    def zb_copy(way, m, stream, src=None):
        return copy(zb_out.at[way, m, stream] if src is None else src, zb_in.at[way, m, stream],
                    onward[way], zb_s.at[way, m, stream], zb_r.at[way, m, stream])

    def cells(m, known):
        if known and m == 0:
            return ((0, 0),)
        return tuple((toward(way, m), cell(way, m)) for way in (0, 1)
                     if not known or m <= reach(nz, "a", way))

    def ahead(m, known, stage):
        for zo, c in cells(m, known):
            stage(zo, c)

    def b_step(m, known):
        for stream in (0, 1, 2, 3):
            for way in (0, 1):
                limit = reach(nz, stream, way)
                if known and m > limit:
                    continue
                block = mine(stream, toward(way, m), cut, wide_b)
                if known and m == limit:
                    zb_copy(way, m - 1, stream, block).start()
                else:
                    zb_copy(way, m, stream).wait_recv()
                    total = block[...].astype(f32) + zb_in[way, m, stream].astype(f32)
                    zb_out[way, m - 1, stream] = total.astype(bf16)
                    zb_copy(way, m - 1, stream).start()

    def a_step(m, known):
        for way in (0, 1):
            limit = reach(nz, "a", way)
            if known and m > limit:
                continue
            total = stage_3(toward(way, m), cell(way, m))
            if not (known and m == limit):
                za_copy(way, m).wait_recv()
                total = total + za_in[way, m].astype(f32)
            za_out[way, m - 1] = total.astype(bf16)
            za_copy(way, m - 1).start()

    group = lax.axis_index("mp")
    width = grad_x_ref.shape[1]

    def part_copy(i):
        return pltpu.make_async_remote_copy(
            src_ref=part_out.at[i], dst_ref=part_in.at[i], send_sem=part_s.at[i], recv_sem=part_r.at[i],
            device_id={"mp": lax.rem(group + i, peers)}, device_id_type=MESH,
        )

    def share(i):
        row = pl.multiple_of(lax.rem(group + i, peers) * width, width)
        part_out[i] = lax.dot_general(
            d_ref[...], weights_ref[pl.ds(row, width), :], (((1,), (1,)), ((), ())),
            preferred_element_type=f32,
        ).astype(bf16)

    def share_out(i):
        share(i)
        part_copy(i).start()

    greet(index, [lax.rem(group + i, peers) for i in range(1, peers)])
    b_step(top, True)
    ahead(top, True, stage_1)
    ahead(top - 1, True, stage_1)
    ahead(top - 2, True, stage_1)
    ahead(top, True, stage_2)
    b_step(top - 1, True)
    ahead(top - 1, True, stage_2)

    def iterate(m, known):
        if not known or m >= 3:
            b_step(m - 2, known)
            ahead(m - 3, known, stage_1)
        if not known or m >= 2:
            ahead(m - 2, known, stage_2)
        a_step(m, known)
        i = top + 1 - m
        if not known or i < peers:
            share_out(i)

    for m in (top, top - 1):
        iterate(m, True)
    inner = (top - 2) - 4 + 1
    if inner > 0:
        def body(i, carry):
            iterate(top - 2 - i, False)
            return carry

        lax.fori_loop(0, inner, body, 0)
    for m in range(min(top - 2, 3), 2, -1):
        iterate(m, True)

    def b_final(stream):
        total = mine(stream, 0, cut, wide_b)[...].astype(f32)
        for way in (0, 1):
            zb_copy(way, 0, stream).wait_recv()
            total = total + zb_in[way, 0, stream].astype(f32)
        return total

    def bf_copy(part):
        start, size = halves_b[part]
        return copy(b_sum.at[:, pl.ds(start, size)], b_far.at[:, pl.ds(start, size)], side[part],
                    bf_s.at[part], bf_r.at[part])

    def bn_copy(part):
        return copy(b_near_out.at[part], b_near.at[part], side[part], bn_s.at[part], bn_r.at[part])

    b_sum[...] = b_final(2).astype(bf16)
    for part in (0, 1):
        bf_copy(part).start()
    iterate(2, True)
    next_to = (b_final(1), b_final(3))
    own_b = b_final(0)
    for part in (0, 1):
        start, size = halves_b[part]
        rest, rest_size = halves_b[1 - part]
        bf_copy(part).wait_recv()
        total = next_to[part]
        b_near_out[part, :, pl.ds(rest, rest_size)] = total[:, rest:rest + rest_size].astype(bf16)
        b_near_out[part, :, pl.ds(start, size)] = (
            total[:, start:start + size] + b_far[:, pl.ds(start, size)].astype(f32)).astype(bf16)
        bn_copy(part).start()
    iterate(1, True)
    for i in range(top + 1, peers):
        share_out(i)
    share(0)
    grad_x = part_out[0].astype(f32)
    for i in range(1, peers):
        part_copy(i).wait_recv()
        grad_x = grad_x + part_in[i].astype(f32)
    grad_x_ref[...] = grad_x.astype(bf16)
    total = stage_3(0, 0)
    for way in (0, 1):
        za_copy(way, 0).wait_recv()
        total = total + za_in[way, 0].astype(f32)
    out_ref[:, pl.ds(0, cut)] = total
    for part in (0, 1):
        bn_copy(part).wait_recv()
    out_ref[:, pl.ds(cut, wide_b)] = (own_b + b_near[0].astype(f32)) + b_near[1].astype(f32)

    def drain_y(zo, c):
        for part in (0, 1):
            far_copy(zo, c, part).wait_send()
            near_copy(c, part).wait_send()

    def drain(m, known):
        ahead(m, known, drain_y)
        for way in (0, 1):
            for stream in (0, 1, 2, 3):
                if not known or m <= reach(nz, stream, way):
                    zb_copy(way, m - 1, stream).wait_send()
            if not known or m <= reach(nz, "a", way):
                za_copy(way, m - 1).wait_send()

    drain_y(0, 0)

    def drain_body(m, carry):
        drain(m, False)
        return carry

    lax.fori_loop(1, top, drain_body, 0)
    drain(top, True)
    for part in (0, 1):
        bf_copy(part).wait_send()
        bn_copy(part).wait_send()
    for i in range(1, peers):
        part_copy(i).wait_send()


def scatter_sum(whole, d_both, weights, ranks, peers):
    rows, cols = whole.shape[0] // ranks, whole.shape[1]
    nz = ranks // RING_Y
    tiles = cols // 128
    cut = 128 * max(2, round(tiles * 0.633 + 0.2))
    half_a = 128 * ((cut // 128 + 1) // 2)
    wide_b = cols - cut
    half_b = 128 * ((wide_b // 128 + 1) // 2)
    k = nz // 2 + 1
    tokens, width = d_both.shape[0], weights.shape[0] // peers
    bf16 = jnp.bfloat16
    dma = pltpu.SemaphoreType.DMA
    return pl.pallas_call(
        functools.partial(scatter_kernel, nz, peers, cut, half_a, half_b),
        out_shape=(
            jax.ShapeDtypeStruct((rows, cols), jnp.float32),
            jax.ShapeDtypeStruct((tokens, width), bf16),
        ),
        in_specs=[VMEM] * 3,
        out_specs=(VMEM, VMEM),
        scratch_shapes=[
            pltpu.VMEM((peers, tokens, width), bf16),
            pltpu.VMEM((peers, tokens, width), bf16),
            pltpu.VMEM((nz, rows, cut), bf16),
            pltpu.VMEM((nz, 2, rows, cut), bf16),
            pltpu.VMEM((nz, 2, rows, cut), bf16),
            pltpu.VMEM((2, k, rows, cut), bf16),
            pltpu.VMEM((2, k, rows, cut), bf16),
            pltpu.VMEM((2, k, 4, rows, wide_b), bf16),
            pltpu.VMEM((2, k, 4, rows, wide_b), bf16),
            pltpu.VMEM((rows, wide_b), bf16),
            pltpu.VMEM((rows, wide_b), bf16),
            pltpu.VMEM((2, rows, wide_b), bf16),
            pltpu.VMEM((2, rows, wide_b), bf16),
            dma((peers,)), dma((peers,)),
            dma((nz, 2)), dma((nz, 2)), dma((nz, 2)), dma((nz, 2)),
            dma((2, k)), dma((2, k)), dma((2, k, 4)), dma((2, k, 4)),
            dma((2,)), dma((2,)), dma((2,)), dma((2,)),
        ],
        compiler_params=pltpu.CompilerParams(
            collective_id=1, has_side_effects=True, vmem_limit_bytes=48 * 1024 * 1024),
        name="scatter_sum",
    )(whole, d_both, weights)


def on_device(x_in, cotangent, w_gate, w_up, send_counts, recv_counts):
    ranks = lax.axis_size("dp")
    hidden = w_gate.shape[1]
    weights, live_rows = gather_rows(w_gate, w_up, send_counts, recv_counts, ranks)
    live = (lax.broadcasted_iota(jnp.float32, (x_in.shape[0], 1), 0) < live_rows[0, 0])
    both = jnp.dot(x_in, weights, preferred_element_type=jnp.float32)
    gate_val, up_val = both[:, :hidden], both[:, hidden:]
    sig = jax.nn.sigmoid(gate_val)
    cot_val = cotangent.astype(jnp.float32)
    d_gate = jnp.where(
        live, cot_val * up_val * sig * (1.0 + gate_val * (1.0 - sig)), 0.0
    ).astype(jnp.bfloat16)
    d_up = jnp.where(live, cot_val * gate_val * sig, 0.0).astype(jnp.bfloat16)
    whole = lax.dot_general(
        x_in, d_gate, (((0,), (0,)), ((), ())), preferred_element_type=jnp.float32
    ).astype(jnp.bfloat16)
    grad_gate, grad_x = scatter_sum(
        whole, jnp.concatenate([d_gate, d_up], axis=1), weights, ranks, lax.axis_size("mp"))
    return (grad_x, grad_gate)


def solution(mesh):
    return jax.shard_map(
        on_device,
        mesh=mesh,
        in_specs=(
            P("dp", None),
            P("dp", "mp"),
            P("dp", "mp"),
            P("dp", "mp"),
            P("dp", None),
            P("dp", None),
        ),
        out_specs=(P("dp", "mp"), P("dp", "mp")),
        check_vma=False,
    )
```

```python
import functools

import jax
import jax.numpy as jnp
from jax import lax
from jax.experimental import pallas as pl
from jax.experimental.pallas import tpu as pltpu
from jax.sharding import PartitionSpec as P

BAL = 208
RING_Y = 4
MESH = pl.DeviceIdType.MESH
VMEM = pl.BlockSpec(memory_space=pltpu.VMEM)


def place(nz):
    me = lax.axis_index("dp")
    y, z = lax.div(me, nz), lax.rem(me, nz)

    def index(yo, zo):
        return lax.rem(y + yo + 2 * RING_Y, RING_Y) * nz + lax.rem(z + zo + 2 * nz, nz)

    return index


def greet(index, peers=()):
    barrier = pltpu.get_barrier_semaphore()
    for peer in peers:
        pl.semaphore_signal(barrier, inc=1, device_id={"mp": peer}, device_id_type=MESH)
    for yo, zo in ((0, 1), (0, -1), (1, 0), (-1, 0)):
        pl.semaphore_signal(
            barrier, inc=1, device_id={"dp": index(yo, zo)}, device_id_type=MESH
        )
    pl.semaphore_wait(barrier, 4 + len(peers))


def reach(nz, stream, way):
    forward = stream in ("a", 0)
    return nz // 2 if forward == (way == 0) else nz // 2 - 1


def gather_kernel(
    nz, cut, half_a, half_b, gate_ref, up_ref, sent_ref, got_ref, cot_ref, out_ref, cot_live_ref,
    w_ref, za_s, za_r, zb_s, zb_r, ya_s, ya_r, yb_s, yb_r, own
):
    index = place(nz)
    rows, cols = w_ref.shape
    top = nz // 2
    spans = {"a": (0, cut), "b": (cut, cols - cut)}
    halves = {
        "a": ((0, half_a), (half_a, cut - half_a)),
        "a_odd": ((half_a, cut - half_a), (0, half_a)),
        "b": ((cut, half_b), (cut + half_b, cols - cut - half_b)),
    }

    def block(yo, zo, span):
        start = pl.multiple_of(index(yo, zo) * rows, rows)
        return out_ref.at[pl.ds(start, rows), pl.ds(span[0], span[1])]

    def copy(src, dst, target, s_sem, r_sem):
        return pltpu.make_async_remote_copy(
            src_ref=src, dst_ref=dst, send_sem=s_sem, recv_sem=r_sem,
            device_id={"dp": index(*target)}, device_id_type=MESH,
        )

    def origin(way, k):
        return -k if way == 0 else k

    def onward(way):
        return (0, 1) if way == 0 else (0, -1)

    def z_copy(stream, way, k, mine=False):
        span = spans["a"] if stream == "a" else spans["b"]
        yo = 0 if stream == "a" else stream
        dst = block(yo, origin(way, k - 1), span)
        src = w_ref.at[:, pl.ds(span[0], span[1])] if mine else dst
        sems = (za_s.at[way, k], za_r.at[way, k]) if stream == "a" else (
            zb_s.at[way, k, stream], zb_r.at[way, k, stream])
        return copy(src, dst, onward(way), *sems)

    def z_wait(stream, way, k):
        span = spans["a"] if stream == "a" else spans["b"]
        yo = 0 if stream == "a" else stream
        dst = block(yo, origin(way, k), span)
        sem = za_r.at[way, k] if stream == "a" else zb_r.at[way, k, stream]
        other = za_s.at[way, k] if stream == "a" else zb_s.at[way, k, stream]
        copy(dst, dst, onward(way), other, sem).wait_recv()

    def y_sems(kind, c, part):
        if kind != "b":
            return ya_s.at[c, part], ya_r.at[c, part]
        return yb_s.at[part], yb_r.at[part]

    def y_part(kind, part):
        return spans[kind[0]] if part < 2 else halves[kind][part - 2]

    def y_copy(kind, zo, c, part, mine=False):
        span = y_part(kind, part)
        yo = 0 if part < 2 else (-1 if part == 2 else 1)
        dst = block(yo, zo, span)
        src = w_ref.at[:, pl.ds(span[0], span[1])] if mine else dst
        return copy(src, dst, (1, 0) if part % 2 == 0 else (-1, 0), *y_sems(kind, c, part))

    def y_wait(kind, zo, c, part):
        yo = (-1, 1, -2, 2)[part]
        dst = block(yo, zo, y_part(kind, part))
        copy(dst, dst, (1, 0), *y_sems(kind, c, part)).wait_recv()

    def cell(way, k):
        return 2 * k - 1 + way

    def sort(way):
        return ("a_odd", "a")[way]

    def y_pass(kind, zo, c):
        for part in (0, 1):
            y_wait(kind, zo, c, part)
            y_copy(kind, zo, c, part + 2).start()

    hidden = gate_ref.shape[1]
    w_ref[:, pl.ds(0, hidden)] = gate_ref[...]
    w_ref[:, pl.ds(hidden, hidden)] = up_ref[...]
    greet(index)
    keep = pltpu.make_async_copy(w_ref, out_ref.at[pl.ds(pl.multiple_of(index(0, 0) * rows, rows), rows), :], own)
    keep.start()
    for part in (0, 1):
        y_copy("b", 0, 0, part, True).start()
    for way in (0, 1):
        z_copy("a", way, 1, True).start()
    for part in (0, 1):
        y_copy("a", 0, 0, part, True).start()
    for way in (0, 1):
        z_copy(0, way, 1, True).start()

    def move(stream, way, k, known):
        if known and k > reach(nz, stream, way):
            return False
        z_wait(stream, way, k)
        if not known or k + 1 <= reach(nz, stream, way):
            z_copy(stream, way, k + 1).start()
        return True

    def a_step(k, known):
        for way in (0, 1):
            if move("a", way, k, known):
                for part in (0, 1):
                    y_copy(sort(way), origin(way, k), cell(way, k), part).start()

    def a_pass(k, known):
        for way in (0, 1):
            if not known or k <= reach(nz, "a", way):
                y_pass(sort(way), origin(way, k), cell(way, k))

    def b_step(k, known):
        for stream in (0, 3, 1, 2):
            for way in (0, 1):
                move(stream, way, k, known)

    change = jnp.sum((sent_ref[...] - got_ref[...]).astype(jnp.float32), axis=1, keepdims=True)
    row = lax.broadcasted_iota(jnp.int32, (cot_ref.shape[0], 128), 0).astype(jnp.float32)
    live = row < jnp.broadcast_to(change + BAL, row.shape)
    for start in range(0, cot_ref.shape[1], 128):
        value = cot_ref[:, pl.ds(start, 128)].astype(jnp.float32)
        cot_live_ref[:, pl.ds(start, 128)] = jnp.where(live, value, 0.0).astype(cot_live_ref.dtype)

    a_step(1, True)
    for part in (0, 1):
        y_wait("b", 0, 0, part)
        y_copy("b", 0, 0, part + 2).start()
        for way in (0, 1):
            z_copy(3 if part == 0 else 1, way, 1).start()
    y_pass("a", 0, 0)
    a_step(2, top > 2 and 2 >= top - 1 or top == 2)
    for part in (2, 3):
        y_wait("b", 0, 0, part)
    for way in (0, 1):
        z_copy(2, way, 1).start()
    a_pass(1, True)

    def body(k, carry):
        a_step(k, False)
        b_step(k - 2, False)
        a_pass(k - 1, False)
        return carry

    if top > 4:
        lax.fori_loop(3, top - 1, body, 0)
    for k in range(max(3, top - 1), top + 1):
        a_step(k, True)
        b_step(k - 2, True)
        a_pass(k - 1, True)
    a_pass(top, True)
    b_step(top - 1, True)
    b_step(top, True)

    def drain_y(kind, c, zo):
        for part in (2, 3):
            y_wait(kind, zo, c, part)
        for part in range(4):
            y_copy(kind, zo, c, part).wait_send()

    drain_y("a", 0, 0)
    for part in range(4):
        y_copy("b", 0, 0, part).wait_send()

    def drain(k, known):
        for way in (0, 1):
            for stream in ("a", 0, 1, 2, 3):
                if not known or k <= reach(nz, stream, way):
                    z_copy(stream, way, k).wait_send()
            if not known or k <= reach(nz, "a", way):
                drain_y(sort(way), cell(way, k), origin(way, k))

    def drain_body(k, carry):
        drain(k, False)
        return carry

    lax.fori_loop(1, top, drain_body, 0)
    drain(top, True)
    keep.wait()


def gather_rows(w_gate, w_up, sent, got, cotangent, ranks):
    rows, cols = w_gate.shape[0], 2 * w_gate.shape[1]
    nz = ranks // RING_Y
    tiles = cols // 128
    cut = 128 * max(2, round(tiles * 0.633))
    half_a = 128 * ((cut // 128 + 1) // 2)
    half_b = 128 * (((cols - cut) // 128 + 1) // 2)
    dma = pltpu.SemaphoreType.DMA
    k = nz // 2 + 1
    return pl.pallas_call(
        functools.partial(gather_kernel, nz, cut, half_a, half_b),
        out_shape=(
            jax.ShapeDtypeStruct((ranks * rows, cols), w_gate.dtype),
            jax.ShapeDtypeStruct(cotangent.shape, cotangent.dtype),
        ),
        in_specs=[VMEM] * 5,
        out_specs=(VMEM, VMEM),
        scratch_shapes=[
            pltpu.VMEM((rows, cols), w_gate.dtype),
            dma((2, k)), dma((2, k)), dma((2, k, 4)), dma((2, k, 4)),
            dma((nz, 4)), dma((nz, 4)), dma((4,)), dma((4,)), dma,
        ],
        compiler_params=pltpu.CompilerParams(
            collective_id=0, has_side_effects=True, vmem_limit_bytes=20 * 1024 * 1024),
        name="gather_rows",
    )(w_gate, w_up, sent, got, cotangent)


def scatter_kernel(
    nz, peers, cut, half_a, half_b, p_ref, d_ref, weights_ref, out_ref, grad_x_ref, part_out, part_in,
    far, near, near_out, za_in, za_out, zb_in, zb_out, b_sum, b_far, b_near, b_near_out,
    part_s, part_r, far_s, far_r, near_s, near_r, za_s, za_r, zb_s, zb_r, bf_s, bf_r, bn_s, bn_r,
):
    index = place(nz)
    rows, cols = out_ref.shape
    top = nz // 2
    f32, bf16 = jnp.float32, jnp.bfloat16
    wide_b = cols - cut
    halves_a = ((0, half_a), (half_a, cut - half_a))
    halves_b = ((0, half_b), (half_b, wide_b - half_b))

    def mine(yo, zo, start, size):
        row = pl.multiple_of(index(yo, zo) * rows, rows)
        return p_ref.at[pl.ds(row, rows), pl.ds(start, size)]

    def copy(src, dst, target, s_sem, r_sem):
        return pltpu.make_async_remote_copy(
            src_ref=src, dst_ref=dst, send_sem=s_sem, recv_sem=r_sem,
            device_id={"dp": index(*target)}, device_id_type=MESH,
        )

    side = ((1, 0), (-1, 0))
    onward = ((0, 1), (0, -1))

    def toward(way, m):
        return m if way == 0 else -m

    def cell(way, m):
        return 2 * m - 1 + way

    def far_copy(zo, c, part):
        start, size = halves_a[part]
        return copy(mine(2, zo, start, size), far.at[c, :, pl.ds(start, size)], side[part],
                    far_s.at[c, part], far_r.at[c, part])

    def near_copy(c, part):
        return copy(near_out.at[c, part], near.at[c, part], side[part],
                    near_s.at[c, part], near_r.at[c, part])

    def stage_1(zo, c):
        for part in (0, 1):
            far_copy(zo, c, part).start()

    def stage_2(zo, c):
        for part in (0, 1):
            start, size = halves_a[part]
            rest, rest_size = halves_a[1 - part]
            yo = 1 if part == 0 else -1
            near_out[c, part, :, pl.ds(rest, rest_size)] = mine(yo, zo, rest, rest_size)[...]
            far_copy(zo, c, part).wait_recv()
            total = mine(yo, zo, start, size)[...].astype(f32) + far[c, :, pl.ds(start, size)].astype(f32)
            near_out[c, part, :, pl.ds(start, size)] = total.astype(bf16)
            near_copy(c, part).start()

    def stage_3(zo, c):
        for part in (0, 1):
            near_copy(c, part).wait_recv()
        return (mine(0, zo, 0, cut)[...].astype(f32) + near[c, 0].astype(f32)) + near[c, 1].astype(f32)

    def za_copy(way, m):
        return copy(za_out.at[way, m], za_in.at[way, m], onward[way], za_s.at[way, m], za_r.at[way, m])

    def zb_copy(way, m, stream, src=None):
        return copy(zb_out.at[way, m, stream] if src is None else src, zb_in.at[way, m, stream],
                    onward[way], zb_s.at[way, m, stream], zb_r.at[way, m, stream])

    def cells(m, known):
        if known and m == 0:
            return ((0, 0),)
        return tuple((toward(way, m), cell(way, m)) for way in (0, 1)
                     if not known or m <= reach(nz, "a", way))

    def ahead(m, known, stage):
        for zo, c in cells(m, known):
            stage(zo, c)

    def b_step(m, known):
        for stream in (0, 1, 2, 3):
            for way in (0, 1):
                limit = reach(nz, stream, way)
                if known and m > limit:
                    continue
                block = mine(stream, toward(way, m), cut, wide_b)
                if known and m == limit:
                    zb_copy(way, m - 1, stream, block).start()
                else:
                    zb_copy(way, m, stream).wait_recv()
                    total = block[...].astype(f32) + zb_in[way, m, stream].astype(f32)
                    zb_out[way, m - 1, stream] = total.astype(bf16)
                    zb_copy(way, m - 1, stream).start()

    def a_step(m, known):
        for way in (0, 1):
            limit = reach(nz, "a", way)
            if known and m > limit:
                continue
            total = stage_3(toward(way, m), cell(way, m))
            if not (known and m == limit):
                za_copy(way, m).wait_recv()
                total = total + za_in[way, m].astype(f32)
            za_out[way, m - 1] = total.astype(bf16)
            za_copy(way, m - 1).start()

    group = lax.axis_index("mp")
    width = grad_x_ref.shape[1]

    def part_copy(i):
        return pltpu.make_async_remote_copy(
            src_ref=part_out.at[i], dst_ref=part_in.at[i], send_sem=part_s.at[i], recv_sem=part_r.at[i],
            device_id={"mp": lax.rem(group + i, peers)}, device_id_type=MESH,
        )

    def share(i):
        row = pl.multiple_of(lax.rem(group + i, peers) * width, width)
        part_out[i] = lax.dot_general(
            d_ref[...], weights_ref[pl.ds(row, width), :], (((1,), (1,)), ((), ())),
            preferred_element_type=f32,
        ).astype(bf16)

    def share_out(i):
        share(i)
        part_copy(i).start()

    greet(index, [lax.rem(group + i, peers) for i in range(1, peers)])
    b_step(top, True)
    ahead(top, True, stage_1)
    ahead(top - 1, True, stage_1)
    ahead(top - 2, True, stage_1)
    ahead(top, True, stage_2)
    b_step(top - 1, True)
    ahead(top - 1, True, stage_2)

    def iterate(m, known):
        if not known or m >= 3:
            b_step(m - 2, known)
            ahead(m - 3, known, stage_1)
        if not known or m >= 2:
            ahead(m - 2, known, stage_2)
        a_step(m, known)
        i = top + 1 - m
        if not known or i < peers:
            share_out(i)

    for m in (top, top - 1):
        iterate(m, True)
    inner = (top - 2) - 4 + 1
    if inner > 0:
        def body(i, carry):
            iterate(top - 2 - i, False)
            return carry

        lax.fori_loop(0, inner, body, 0)
    for m in range(min(top - 2, 3), 2, -1):
        iterate(m, True)

    def b_final(stream):
        total = mine(stream, 0, cut, wide_b)[...].astype(f32)
        for way in (0, 1):
            zb_copy(way, 0, stream).wait_recv()
            total = total + zb_in[way, 0, stream].astype(f32)
        return total

    def bf_copy(part):
        start, size = halves_b[part]
        return copy(b_sum.at[:, pl.ds(start, size)], b_far.at[:, pl.ds(start, size)], side[part],
                    bf_s.at[part], bf_r.at[part])

    def bn_copy(part):
        return copy(b_near_out.at[part], b_near.at[part], side[part], bn_s.at[part], bn_r.at[part])

    b_sum[...] = b_final(2).astype(bf16)
    for part in (0, 1):
        bf_copy(part).start()
    iterate(2, True)
    next_to = (b_final(1), b_final(3))
    own_b = b_final(0)
    for part in (0, 1):
        start, size = halves_b[part]
        rest, rest_size = halves_b[1 - part]
        bf_copy(part).wait_recv()
        total = next_to[part]
        b_near_out[part, :, pl.ds(rest, rest_size)] = total[:, rest:rest + rest_size].astype(bf16)
        b_near_out[part, :, pl.ds(start, size)] = (
            total[:, start:start + size] + b_far[:, pl.ds(start, size)].astype(f32)).astype(bf16)
        bn_copy(part).start()
    iterate(1, True)
    for i in range(top + 1, peers):
        share_out(i)
    share(0)
    grad_x = part_out[0].astype(f32)
    for i in range(1, peers):
        part_copy(i).wait_recv()
        grad_x = grad_x + part_in[i].astype(f32)
    grad_x_ref[...] = grad_x.astype(bf16)
    total = stage_3(0, 0)
    for way in (0, 1):
        za_copy(way, 0).wait_recv()
        total = total + za_in[way, 0].astype(f32)
    out_ref[:, pl.ds(0, cut)] = total
    for part in (0, 1):
        bn_copy(part).wait_recv()
    out_ref[:, pl.ds(cut, wide_b)] = (own_b + b_near[0].astype(f32)) + b_near[1].astype(f32)

    def drain_y(zo, c):
        for part in (0, 1):
            far_copy(zo, c, part).wait_send()
            near_copy(c, part).wait_send()

    def drain(m, known):
        ahead(m, known, drain_y)
        for way in (0, 1):
            for stream in (0, 1, 2, 3):
                if not known or m <= reach(nz, stream, way):
                    zb_copy(way, m - 1, stream).wait_send()
            if not known or m <= reach(nz, "a", way):
                za_copy(way, m - 1).wait_send()

    drain_y(0, 0)

    def drain_body(m, carry):
        drain(m, False)
        return carry

    lax.fori_loop(1, top, drain_body, 0)
    drain(top, True)
    for part in (0, 1):
        bf_copy(part).wait_send()
        bn_copy(part).wait_send()
    for i in range(1, peers):
        part_copy(i).wait_send()


def scatter_sum(whole, d_both, weights, ranks, peers):
    rows, cols = whole.shape[0] // ranks, whole.shape[1]
    nz = ranks // RING_Y
    tiles = cols // 128
    cut = 128 * max(2, round(tiles * 0.55))
    half_a = 128 * ((cut // 128 + 1) // 2)
    wide_b = cols - cut
    half_b = 128 * ((wide_b // 128 + 1) // 2)
    k = nz // 2 + 1
    tokens, width = d_both.shape[0], weights.shape[0] // peers
    bf16 = jnp.bfloat16
    dma = pltpu.SemaphoreType.DMA
    return pl.pallas_call(
        functools.partial(scatter_kernel, nz, peers, cut, half_a, half_b),
        out_shape=(
            jax.ShapeDtypeStruct((rows, cols), jnp.float32),
            jax.ShapeDtypeStruct((tokens, width), bf16),
        ),
        in_specs=[VMEM] * 3,
        out_specs=(VMEM, VMEM),
        scratch_shapes=[
            pltpu.VMEM((peers, tokens, width), bf16),
            pltpu.VMEM((peers, tokens, width), bf16),
            pltpu.VMEM((nz, rows, cut), bf16),
            pltpu.VMEM((nz, 2, rows, cut), bf16),
            pltpu.VMEM((nz, 2, rows, cut), bf16),
            pltpu.VMEM((2, k, rows, cut), bf16),
            pltpu.VMEM((2, k, rows, cut), bf16),
            pltpu.VMEM((2, k, 4, rows, wide_b), bf16),
            pltpu.VMEM((2, k, 4, rows, wide_b), bf16),
            pltpu.VMEM((rows, wide_b), bf16),
            pltpu.VMEM((rows, wide_b), bf16),
            pltpu.VMEM((2, rows, wide_b), bf16),
            pltpu.VMEM((2, rows, wide_b), bf16),
            dma((peers,)), dma((peers,)),
            dma((nz, 2)), dma((nz, 2)), dma((nz, 2)), dma((nz, 2)),
            dma((2, k)), dma((2, k)), dma((2, k, 4)), dma((2, k, 4)),
            dma((2,)), dma((2,)), dma((2,)), dma((2,)),
        ],
        compiler_params=pltpu.CompilerParams(
            collective_id=1, has_side_effects=True, vmem_limit_bytes=32 * 1024 * 1024),
        name="scatter_sum",
    )(whole, d_both, weights)


def on_device(x_in, cotangent, w_gate, w_up, send_counts, recv_counts):
    ranks = lax.axis_size("dp")
    hidden = w_gate.shape[1]
    weights, cot_live = gather_rows(w_gate, w_up, send_counts, recv_counts, cotangent, ranks)
    both = jnp.dot(x_in, weights, preferred_element_type=jnp.float32)
    gate_val, up_val = both[:, :hidden], both[:, hidden:]
    sig = jax.nn.sigmoid(gate_val)
    cot_val = cot_live.astype(jnp.float32)
    d_gate = (cot_val * up_val * sig * (1.0 + gate_val * (1.0 - sig))).astype(jnp.bfloat16)
    d_up = (cot_val * gate_val * sig).astype(jnp.bfloat16)
    whole = lax.dot_general(
        x_in, d_gate, (((0,), (0,)), ((), ())), preferred_element_type=jnp.float32
    ).astype(jnp.bfloat16)
    grad_gate, grad_x = scatter_sum(
        whole, jnp.concatenate([d_gate, d_up], axis=1), weights, ranks, lax.axis_size("mp"))
    return (grad_x, grad_gate)


def solution(mesh):
    return jax.shard_map(
        on_device,
        mesh=mesh,
        in_specs=(
            P("dp", None),
            P("dp", "mp"),
            P("dp", "mp"),
            P("dp", "mp"),
            P("dp", None),
            P("dp", None),
        ),
        out_specs=(P("dp", "mp"), P("dp", "mp")),
        check_vma=False,
    )
```

```python
import functools

import jax
import jax.numpy as jnp
from jax import lax
from jax.experimental import pallas as pl
from jax.experimental.pallas import tpu as pltpu
from jax.sharding import PartitionSpec as P

BAL = 208
RING_Y = 4
MESH = pl.DeviceIdType.MESH
VMEM = pl.BlockSpec(memory_space=pltpu.VMEM)
HBM = pl.BlockSpec(memory_space=pltpu.HBM)


def place(nz):
    me = lax.axis_index("dp")
    y, z = lax.div(me, nz), lax.rem(me, nz)

    def index(yo, zo):
        return lax.rem(y + yo + 2 * RING_Y, RING_Y) * nz + lax.rem(z + zo + 2 * nz, nz)

    return index


def greet(index, peers=()):
    barrier = pltpu.get_barrier_semaphore()
    for peer in peers:
        pl.semaphore_signal(barrier, inc=1, device_id={"mp": peer}, device_id_type=MESH)
    for yo, zo in ((0, 1), (0, -1), (1, 0), (-1, 0)):
        pl.semaphore_signal(
            barrier, inc=1, device_id={"dp": index(yo, zo)}, device_id_type=MESH
        )
    pl.semaphore_wait(barrier, 4 + len(peers))


def reach(nz, stream, way):
    forward = stream in ("a", 0)
    return nz // 2 if forward == (way == 0) else nz // 2 - 1


def gather_kernel(
    nz, cut, half_a, half_b, gate_ref, up_ref, sent_hbm, got_hbm, cot_hbm, out_ref, cot_live_ref,
    w_ref, sent_ref, got_ref, cot_ref, fetched,
    za_s, za_r, zb_s, zb_r, ya_s, ya_r, yb_s, yb_r, own
):
    index = place(nz)
    rows, cols = w_ref.shape
    top = nz // 2
    spans = {"a": (0, cut), "b": (cut, cols - cut)}
    halves = {
        "a": ((0, half_a), (half_a, cut - half_a)),
        "a_odd": ((half_a, cut - half_a), (0, half_a)),
        "b": ((cut, half_b), (cut + half_b, cols - cut - half_b)),
    }

    def block(yo, zo, span):
        start = pl.multiple_of(index(yo, zo) * rows, rows)
        return out_ref.at[pl.ds(start, rows), pl.ds(span[0], span[1])]

    def copy(src, dst, target, s_sem, r_sem):
        return pltpu.make_async_remote_copy(
            src_ref=src, dst_ref=dst, send_sem=s_sem, recv_sem=r_sem,
            device_id={"dp": index(*target)}, device_id_type=MESH,
        )

    def origin(way, k):
        return -k if way == 0 else k

    def onward(way):
        return (0, 1) if way == 0 else (0, -1)

    def z_copy(stream, way, k, mine=False):
        span = spans["a"] if stream == "a" else spans["b"]
        yo = 0 if stream == "a" else stream
        dst = block(yo, origin(way, k - 1), span)
        src = w_ref.at[:, pl.ds(span[0], span[1])] if mine else dst
        sems = (za_s.at[way, k], za_r.at[way, k]) if stream == "a" else (
            zb_s.at[way, k, stream], zb_r.at[way, k, stream])
        return copy(src, dst, onward(way), *sems)

    def z_wait(stream, way, k):
        span = spans["a"] if stream == "a" else spans["b"]
        yo = 0 if stream == "a" else stream
        dst = block(yo, origin(way, k), span)
        sem = za_r.at[way, k] if stream == "a" else zb_r.at[way, k, stream]
        other = za_s.at[way, k] if stream == "a" else zb_s.at[way, k, stream]
        copy(dst, dst, onward(way), other, sem).wait_recv()

    def y_sems(kind, c, part):
        if kind != "b":
            return ya_s.at[c, part], ya_r.at[c, part]
        return yb_s.at[part], yb_r.at[part]

    def y_part(kind, part):
        return spans[kind[0]] if part < 2 else halves[kind][part - 2]

    def y_copy(kind, zo, c, part, mine=False):
        span = y_part(kind, part)
        yo = 0 if part < 2 else (-1 if part == 2 else 1)
        dst = block(yo, zo, span)
        src = w_ref.at[:, pl.ds(span[0], span[1])] if mine else dst
        return copy(src, dst, (1, 0) if part % 2 == 0 else (-1, 0), *y_sems(kind, c, part))

    def y_wait(kind, zo, c, part):
        yo = (-1, 1, -2, 2)[part]
        dst = block(yo, zo, y_part(kind, part))
        copy(dst, dst, (1, 0), *y_sems(kind, c, part)).wait_recv()

    def cell(way, k):
        return 2 * k - 1 + way

    def sort(way):
        return ("a_odd", "a")[way]

    def y_pass(kind, zo, c):
        for part in (0, 1):
            y_wait(kind, zo, c, part)
            y_copy(kind, zo, c, part + 2).start()

    hidden = gate_ref.shape[1]
    fetches = [
        pltpu.make_async_copy(src, dst, fetched.at[i])
        for i, (src, dst) in enumerate((
            (gate_ref, w_ref.at[:, pl.ds(0, hidden)]),
            (up_ref, w_ref.at[:, pl.ds(hidden, hidden)]),
            (sent_hbm, sent_ref),
            (got_hbm, got_ref),
            (cot_hbm, cot_ref),
        ))
    ]
    for fetch in fetches:
        fetch.start()
    greet(index)
    for fetch in fetches[:2]:
        fetch.wait()
    keep = pltpu.make_async_copy(w_ref, out_ref.at[pl.ds(pl.multiple_of(index(0, 0) * rows, rows), rows), :], own)
    keep.start()
    for part in (0, 1):
        y_copy("b", 0, 0, part, True).start()
    for way in (0, 1):
        z_copy("a", way, 1, True).start()
    for part in (0, 1):
        y_copy("a", 0, 0, part, True).start()
    for way in (0, 1):
        z_copy(0, way, 1, True).start()

    def move(stream, way, k, known):
        if known and k > reach(nz, stream, way):
            return False
        z_wait(stream, way, k)
        if not known or k + 1 <= reach(nz, stream, way):
            z_copy(stream, way, k + 1).start()
        return True

    def a_step(k, known):
        for way in (0, 1):
            if move("a", way, k, known):
                for part in (0, 1):
                    y_copy(sort(way), origin(way, k), cell(way, k), part).start()

    def a_pass(k, known):
        for way in (0, 1):
            if not known or k <= reach(nz, "a", way):
                y_pass(sort(way), origin(way, k), cell(way, k))

    def b_step(k, known):
        for stream in (0, 3, 1, 2):
            for way in (0, 1):
                move(stream, way, k, known)

    for fetch in fetches[2:]:
        fetch.wait()
    change = jnp.sum((sent_ref[...] - got_ref[...]).astype(jnp.float32), axis=1, keepdims=True)
    row = lax.broadcasted_iota(jnp.int32, (cot_ref.shape[0], 128), 0).astype(jnp.float32)
    live = row < jnp.broadcast_to(change + BAL, row.shape)
    for start in range(0, cot_ref.shape[1], 128):
        value = cot_ref[:, pl.ds(start, 128)].astype(jnp.float32)
        cot_live_ref[:, pl.ds(start, 128)] = jnp.where(live, value, 0.0).astype(cot_live_ref.dtype)

    a_step(1, True)
    for part in (0, 1):
        y_wait("b", 0, 0, part)
        y_copy("b", 0, 0, part + 2).start()
        for way in (0, 1):
            z_copy(3 if part == 0 else 1, way, 1).start()
    y_pass("a", 0, 0)
    a_step(2, top > 2 and 2 >= top - 1 or top == 2)
    for part in (2, 3):
        y_wait("b", 0, 0, part)
    for way in (0, 1):
        z_copy(2, way, 1).start()
    a_pass(1, True)

    def body(k, carry):
        a_step(k, False)
        b_step(k - 2, False)
        a_pass(k - 1, False)
        return carry

    if top > 4:
        lax.fori_loop(3, top - 1, body, 0)
    for k in range(max(3, top - 1), top + 1):
        a_step(k, True)
        b_step(k - 2, True)
        a_pass(k - 1, True)
    a_pass(top, True)
    b_step(top - 1, True)
    b_step(top, True)

    def drain_y(kind, c, zo):
        for part in (2, 3):
            y_wait(kind, zo, c, part)
        for part in range(4):
            y_copy(kind, zo, c, part).wait_send()

    drain_y("a", 0, 0)
    for part in range(4):
        y_copy("b", 0, 0, part).wait_send()

    def drain(k, known):
        for way in (0, 1):
            for stream in ("a", 0, 1, 2, 3):
                if not known or k <= reach(nz, stream, way):
                    z_copy(stream, way, k).wait_send()
            if not known or k <= reach(nz, "a", way):
                drain_y(sort(way), cell(way, k), origin(way, k))

    def drain_body(k, carry):
        drain(k, False)
        return carry

    lax.fori_loop(1, top, drain_body, 0)
    drain(top, True)
    keep.wait()


def gather_rows(w_gate, w_up, sent, got, cotangent, ranks):
    rows, cols = w_gate.shape[0], 2 * w_gate.shape[1]
    nz = ranks // RING_Y
    tiles = cols // 128
    cut = 128 * max(2, round(tiles * 0.633))
    half_a = 128 * ((cut // 128 + 1) // 2)
    half_b = 128 * (((cols - cut) // 128 + 1) // 2)
    dma = pltpu.SemaphoreType.DMA
    k = nz // 2 + 1
    return pl.pallas_call(
        functools.partial(gather_kernel, nz, cut, half_a, half_b),
        out_shape=(
            jax.ShapeDtypeStruct((ranks * rows, cols), w_gate.dtype),
            jax.ShapeDtypeStruct(cotangent.shape, cotangent.dtype),
        ),
        in_specs=[HBM] * 5,
        out_specs=(VMEM, VMEM),
        scratch_shapes=[
            pltpu.VMEM((rows, cols), w_gate.dtype),
            pltpu.VMEM(sent.shape, sent.dtype),
            pltpu.VMEM(got.shape, got.dtype),
            pltpu.VMEM(cotangent.shape, cotangent.dtype),
            dma((5,)),
            dma((2, k)), dma((2, k)), dma((2, k, 4)), dma((2, k, 4)),
            dma((nz, 4)), dma((nz, 4)), dma((4,)), dma((4,)), dma,
        ],
        compiler_params=pltpu.CompilerParams(
            collective_id=0, has_side_effects=True, vmem_limit_bytes=20 * 1024 * 1024),
        name="gather_rows",
    )(*(pltpu.with_memory_space_constraint(a, pltpu.HBM) for a in (w_gate, w_up, sent, got, cotangent)))


def scatter_kernel(
    nz, peers, cut, half_a, half_b, p_ref, d_ref, weights_ref, out_ref, grad_x_ref, part_out, part_in,
    far, near, near_out, za_in, za_out, zb_in, zb_out, b_sum, b_far, b_near, b_near_out,
    part_s, part_r, far_s, far_r, near_s, near_r, za_s, za_r, zb_s, zb_r, bf_s, bf_r, bn_s, bn_r,
):
    index = place(nz)
    rows, cols = out_ref.shape
    top = nz // 2
    f32, bf16 = jnp.float32, jnp.bfloat16
    wide_b = cols - cut
    halves_a = ((0, half_a), (half_a, cut - half_a))
    halves_b = ((0, half_b), (half_b, wide_b - half_b))

    def mine(yo, zo, start, size):
        row = pl.multiple_of(index(yo, zo) * rows, rows)
        return p_ref.at[pl.ds(row, rows), pl.ds(start, size)]

    def copy(src, dst, target, s_sem, r_sem):
        return pltpu.make_async_remote_copy(
            src_ref=src, dst_ref=dst, send_sem=s_sem, recv_sem=r_sem,
            device_id={"dp": index(*target)}, device_id_type=MESH,
        )

    side = ((1, 0), (-1, 0))
    onward = ((0, 1), (0, -1))

    def toward(way, m):
        return m if way == 0 else -m

    def cell(way, m):
        return 2 * m - 1 + way

    def far_copy(zo, c, part):
        start, size = halves_a[part]
        return copy(mine(2, zo, start, size), far.at[c, :, pl.ds(start, size)], side[part],
                    far_s.at[c, part], far_r.at[c, part])

    def near_copy(c, part):
        return copy(near_out.at[c, part], near.at[c, part], side[part],
                    near_s.at[c, part], near_r.at[c, part])

    def stage_1(zo, c):
        for part in (0, 1):
            far_copy(zo, c, part).start()

    def stage_2(zo, c):
        for part in (0, 1):
            start, size = halves_a[part]
            rest, rest_size = halves_a[1 - part]
            yo = 1 if part == 0 else -1
            near_out[c, part, :, pl.ds(rest, rest_size)] = mine(yo, zo, rest, rest_size)[...]
            far_copy(zo, c, part).wait_recv()
            total = mine(yo, zo, start, size)[...].astype(f32) + far[c, :, pl.ds(start, size)].astype(f32)
            near_out[c, part, :, pl.ds(start, size)] = total.astype(bf16)
            near_copy(c, part).start()

    def stage_3(zo, c):
        for part in (0, 1):
            near_copy(c, part).wait_recv()
        return (mine(0, zo, 0, cut)[...].astype(f32) + near[c, 0].astype(f32)) + near[c, 1].astype(f32)

    def za_copy(way, m):
        return copy(za_out.at[way, m], za_in.at[way, m], onward[way], za_s.at[way, m], za_r.at[way, m])

    def zb_copy(way, m, stream, src=None):
        return copy(zb_out.at[way, m, stream] if src is None else src, zb_in.at[way, m, stream],
                    onward[way], zb_s.at[way, m, stream], zb_r.at[way, m, stream])

    def cells(m, known):
        if known and m == 0:
            return ((0, 0),)
        return tuple((toward(way, m), cell(way, m)) for way in (0, 1)
                     if not known or m <= reach(nz, "a", way))

    def ahead(m, known, stage):
        for zo, c in cells(m, known):
            stage(zo, c)

    def b_step(m, known):
        for stream in (0, 1, 2, 3):
            for way in (0, 1):
                limit = reach(nz, stream, way)
                if known and m > limit:
                    continue
                block = mine(stream, toward(way, m), cut, wide_b)
                if known and m == limit:
                    zb_copy(way, m - 1, stream, block).start()
                else:
                    zb_copy(way, m, stream).wait_recv()
                    total = block[...].astype(f32) + zb_in[way, m, stream].astype(f32)
                    zb_out[way, m - 1, stream] = total.astype(bf16)
                    zb_copy(way, m - 1, stream).start()

    def a_step(m, known):
        for way in (0, 1):
            limit = reach(nz, "a", way)
            if known and m > limit:
                continue
            total = stage_3(toward(way, m), cell(way, m))
            if not (known and m == limit):
                za_copy(way, m).wait_recv()
                total = total + za_in[way, m].astype(f32)
            za_out[way, m - 1] = total.astype(bf16)
            za_copy(way, m - 1).start()

    group = lax.axis_index("mp")
    width = grad_x_ref.shape[1]

    chips = peers // 2
    chip, core = lax.div(group, 2), lax.rem(group, 2)

    def owner(j, same):
        return lax.rem(chip + j, chips) * 2 + (core if same else 1 - core)

    def part_copy(i, target):
        return pltpu.make_async_remote_copy(
            src_ref=part_out.at[i], dst_ref=part_in.at[i], send_sem=part_s.at[i], recv_sem=part_r.at[i],
            device_id={"mp": target}, device_id_type=MESH,
        )

    def chip_copy(j):
        return part_copy(j, owner(j, True))

    def pair_copy(j):
        return part_copy(chips + j, owner(0, False))

    def share(i, target):
        row = pl.multiple_of(target * width, width)
        part_out[i] = lax.dot_general(
            d_ref[...], weights_ref[pl.ds(row, width), :], (((1,), (1,)), ((), ())),
            preferred_element_type=f32,
        ).astype(bf16)

    def pair_sum(j):
        pair_copy(j).wait_recv()
        return part_out[j].astype(f32) + part_in[chips + j].astype(f32)

    tour = sorted(range(chips), key=lambda j: -min(j, chips - j))
    jobs = [(j, same) for j in tour for same in (False, True)]
    ready = []

    def advance():
        if ready:
            j = ready.pop(0)
            part_out[j] = pair_sum(j).astype(bf16)
            chip_copy(j).start()
        if jobs:
            j, same = jobs.pop(0)
            share(j if same else chips + j, owner(j, same))
            if not same:
                pair_copy(j).start()
            elif j:
                ready.append(j)

    greet(index, [owner(0, False)] + [owner(j, True) for j in range(1, chips)])
    b_step(top, True)
    ahead(top, True, stage_1)
    ahead(top - 1, True, stage_1)
    ahead(top - 2, True, stage_1)
    advance()
    ahead(top, True, stage_2)
    b_step(top - 1, True)
    advance()
    ahead(top - 1, True, stage_2)

    def iterate(m, known):
        if not known or m >= 3:
            b_step(m - 2, known)
            ahead(m - 3, known, stage_1)
        if not known or m >= 2:
            ahead(m - 2, known, stage_2)
        a_step(m, known)
        advance()

    for m in range(top, 2, -1):
        iterate(m, True)

    def b_final(stream):
        total = mine(stream, 0, cut, wide_b)[...].astype(f32)
        for way in (0, 1):
            zb_copy(way, 0, stream).wait_recv()
            total = total + zb_in[way, 0, stream].astype(f32)
        return total

    def bf_copy(part):
        start, size = halves_b[part]
        return copy(b_sum.at[:, pl.ds(start, size)], b_far.at[:, pl.ds(start, size)], side[part],
                    bf_s.at[part], bf_r.at[part])

    def bn_copy(part):
        return copy(b_near_out.at[part], b_near.at[part], side[part], bn_s.at[part], bn_r.at[part])

    b_sum[...] = b_final(2).astype(bf16)
    for part in (0, 1):
        bf_copy(part).start()
    iterate(2, True)
    next_to = (b_final(1), b_final(3))
    own_b = b_final(0)
    for part in (0, 1):
        start, size = halves_b[part]
        rest, rest_size = halves_b[1 - part]
        bf_copy(part).wait_recv()
        total = next_to[part]
        b_near_out[part, :, pl.ds(rest, rest_size)] = total[:, rest:rest + rest_size].astype(bf16)
        b_near_out[part, :, pl.ds(start, size)] = (
            total[:, start:start + size] + b_far[:, pl.ds(start, size)].astype(f32)).astype(bf16)
        bn_copy(part).start()
    iterate(1, True)
    while jobs or ready:
        advance()
    grad_x = pair_sum(0)
    for j in range(1, chips):
        chip_copy(j).wait_recv()
        grad_x = grad_x + part_in[j].astype(f32)
    grad_x_ref[...] = grad_x.astype(bf16)
    total = stage_3(0, 0)
    for way in (0, 1):
        za_copy(way, 0).wait_recv()
        total = total + za_in[way, 0].astype(f32)
    out_ref[:, pl.ds(0, cut)] = total
    for part in (0, 1):
        bn_copy(part).wait_recv()
    out_ref[:, pl.ds(cut, wide_b)] = (own_b + b_near[0].astype(f32)) + b_near[1].astype(f32)

    def drain_y(zo, c):
        for part in (0, 1):
            far_copy(zo, c, part).wait_send()
            near_copy(c, part).wait_send()

    def drain(m, known):
        ahead(m, known, drain_y)
        for way in (0, 1):
            for stream in (0, 1, 2, 3):
                if not known or m <= reach(nz, stream, way):
                    zb_copy(way, m - 1, stream).wait_send()
            if not known or m <= reach(nz, "a", way):
                za_copy(way, m - 1).wait_send()

    drain_y(0, 0)

    def drain_body(m, carry):
        drain(m, False)
        return carry

    lax.fori_loop(1, top, drain_body, 0)
    drain(top, True)
    for part in (0, 1):
        bf_copy(part).wait_send()
        bn_copy(part).wait_send()
    for j in range(chips):
        pair_copy(j).wait_send()
        if j:
            chip_copy(j).wait_send()


def scatter_sum(whole, d_both, weights, ranks, peers):
    rows, cols = whole.shape[0] // ranks, whole.shape[1]
    nz = ranks // RING_Y
    tiles = cols // 128
    cut = 128 * max(2, round(tiles * 0.55))
    half_a = 128 * ((cut // 128 + 1) // 2)
    wide_b = cols - cut
    half_b = 128 * ((wide_b // 128 + 1) // 2)
    k = nz // 2 + 1
    tokens, width = d_both.shape[0], weights.shape[0] // peers
    bf16 = jnp.bfloat16
    dma = pltpu.SemaphoreType.DMA
    return pl.pallas_call(
        functools.partial(scatter_kernel, nz, peers, cut, half_a, half_b),
        out_shape=(
            jax.ShapeDtypeStruct((rows, cols), jnp.float32),
            jax.ShapeDtypeStruct((tokens, width), bf16),
        ),
        in_specs=[VMEM] * 3,
        out_specs=(VMEM, VMEM),
        scratch_shapes=[
            pltpu.VMEM((peers, tokens, width), bf16),
            pltpu.VMEM((peers, tokens, width), bf16),
            pltpu.VMEM((nz, rows, cut), bf16),
            pltpu.VMEM((nz, 2, rows, cut), bf16),
            pltpu.VMEM((nz, 2, rows, cut), bf16),
            pltpu.VMEM((2, k, rows, cut), bf16),
            pltpu.VMEM((2, k, rows, cut), bf16),
            pltpu.VMEM((2, k, 4, rows, wide_b), bf16),
            pltpu.VMEM((2, k, 4, rows, wide_b), bf16),
            pltpu.VMEM((rows, wide_b), bf16),
            pltpu.VMEM((rows, wide_b), bf16),
            pltpu.VMEM((2, rows, wide_b), bf16),
            pltpu.VMEM((2, rows, wide_b), bf16),
            dma((peers,)), dma((peers,)),
            dma((nz, 2)), dma((nz, 2)), dma((nz, 2)), dma((nz, 2)),
            dma((2, k)), dma((2, k)), dma((2, k, 4)), dma((2, k, 4)),
            dma((2,)), dma((2,)), dma((2,)), dma((2,)),
        ],
        compiler_params=pltpu.CompilerParams(
            collective_id=1, has_side_effects=True, vmem_limit_bytes=32 * 1024 * 1024),
        name="scatter_sum",
    )(whole, d_both, weights)


def on_device(x_in, cotangent, w_gate, w_up, send_counts, recv_counts):
    ranks = lax.axis_size("dp")
    hidden = w_gate.shape[1]
    weights, cot_live = gather_rows(w_gate, w_up, send_counts, recv_counts, cotangent, ranks)
    both = jnp.dot(x_in, weights, preferred_element_type=jnp.float32)
    gate_val, up_val = both[:, :hidden], both[:, hidden:]
    sig = jax.nn.sigmoid(gate_val)
    cot_val = cot_live.astype(jnp.float32)
    d_gate = (cot_val * up_val * sig * (1.0 + gate_val * (1.0 - sig))).astype(jnp.bfloat16)
    d_up = (cot_val * gate_val * sig).astype(jnp.bfloat16)
    whole = lax.dot_general(
        x_in, d_gate, (((0,), (0,)), ((), ())), preferred_element_type=jnp.float32
    ).astype(jnp.bfloat16)
    grad_gate, grad_x = scatter_sum(
        whole, jnp.concatenate([d_gate, d_up], axis=1), weights, ranks, lax.axis_size("mp"))
    return (grad_x, grad_gate)


def solution(mesh):
    return jax.shard_map(
        on_device,
        mesh=mesh,
        in_specs=(
            P("dp", None),
            P("dp", "mp"),
            P("dp", "mp"),
            P("dp", "mp"),
            P("dp", None),
            P("dp", None),
        ),
        out_specs=(P("dp", "mp"), P("dp", "mp")),
        check_vma=False,
    )
```

```python
import functools

import jax
import jax.numpy as jnp
from jax import lax
from jax.experimental import pallas as pl
from jax.experimental.pallas import tpu as pltpu
from jax.sharding import PartitionSpec as P

BAL = 208
RING_Y = 4
MESH = pl.DeviceIdType.MESH
VMEM = pl.BlockSpec(memory_space=pltpu.VMEM)
HBM = pl.BlockSpec(memory_space=pltpu.HBM)


def place(nz):
    me = lax.axis_index("dp")
    y, z = lax.div(me, nz), lax.rem(me, nz)

    def index(yo, zo):
        return lax.rem(y + yo + 2 * RING_Y, RING_Y) * nz + lax.rem(z + zo + 2 * nz, nz)

    return index


def greet(index, peers=()):
    barrier = pltpu.get_barrier_semaphore()
    for peer in peers:
        pl.semaphore_signal(barrier, inc=1, device_id={"mp": peer}, device_id_type=MESH)
    for yo, zo in ((0, 1), (0, -1), (1, 0), (-1, 0)):
        pl.semaphore_signal(
            barrier, inc=1, device_id={"dp": index(yo, zo)}, device_id_type=MESH
        )
    pl.semaphore_wait(barrier, 4 + len(peers))


def reach(nz, stream, way):
    forward = stream in ("a", 0)
    return nz // 2 if forward == (way == 0) else nz // 2 - 1


def gather_kernel(
    nz, cut, half_a, half_b, gate_ref, up_ref, sent_hbm, got_hbm, cot_hbm, out_ref, cot_live_ref,
    w_ref, sent_ref, got_ref, cot_ref, fetched,
    za_s, za_r, zb_s, zb_r, ya_s, ya_r, yb_s, yb_r, own
):
    index = place(nz)
    rows, cols = w_ref.shape
    top = nz // 2
    spans = {"a": (0, cut), "b": (cut, cols - cut)}
    halves = {
        "a": ((0, half_a), (half_a, cut - half_a)),
        "a_odd": ((half_a, cut - half_a), (0, half_a)),
        "b": ((cut, half_b), (cut + half_b, cols - cut - half_b)),
    }

    def block(yo, zo, span):
        start = pl.multiple_of(index(yo, zo) * rows, rows)
        return out_ref.at[pl.ds(start, rows), pl.ds(span[0], span[1])]

    def copy(src, dst, target, s_sem, r_sem):
        return pltpu.make_async_remote_copy(
            src_ref=src, dst_ref=dst, send_sem=s_sem, recv_sem=r_sem,
            device_id={"dp": index(*target)}, device_id_type=MESH,
        )

    def origin(way, k):
        return -k if way == 0 else k

    def onward(way):
        return (0, 1) if way == 0 else (0, -1)

    def z_copy(stream, way, k, mine=False):
        span = spans["a"] if stream == "a" else spans["b"]
        yo = 0 if stream == "a" else stream
        dst = block(yo, origin(way, k - 1), span)
        src = w_ref.at[:, pl.ds(span[0], span[1])] if mine else dst
        sems = (za_s.at[way, k], za_r.at[way, k]) if stream == "a" else (
            zb_s.at[way, k, stream], zb_r.at[way, k, stream])
        return copy(src, dst, onward(way), *sems)

    def z_wait(stream, way, k):
        span = spans["a"] if stream == "a" else spans["b"]
        yo = 0 if stream == "a" else stream
        dst = block(yo, origin(way, k), span)
        sem = za_r.at[way, k] if stream == "a" else zb_r.at[way, k, stream]
        other = za_s.at[way, k] if stream == "a" else zb_s.at[way, k, stream]
        copy(dst, dst, onward(way), other, sem).wait_recv()

    def y_sems(kind, c, part):
        if kind != "b":
            return ya_s.at[c, part], ya_r.at[c, part]
        return yb_s.at[part], yb_r.at[part]

    def y_part(kind, part):
        return spans[kind[0]] if part < 2 else halves[kind][part - 2]

    def y_copy(kind, zo, c, part, mine=False):
        span = y_part(kind, part)
        yo = 0 if part < 2 else (-1 if part == 2 else 1)
        dst = block(yo, zo, span)
        src = w_ref.at[:, pl.ds(span[0], span[1])] if mine else dst
        return copy(src, dst, (1, 0) if part % 2 == 0 else (-1, 0), *y_sems(kind, c, part))

    def y_wait(kind, zo, c, part):
        yo = (-1, 1, -2, 2)[part]
        dst = block(yo, zo, y_part(kind, part))
        copy(dst, dst, (1, 0), *y_sems(kind, c, part)).wait_recv()

    def cell(way, k):
        return 2 * k - 1 + way

    def sort(way):
        return ("a_odd", "a")[way]

    def y_pass(kind, zo, c):
        for part in (0, 1):
            y_wait(kind, zo, c, part)
            y_copy(kind, zo, c, part + 2).start()

    hidden = gate_ref.shape[1]
    fetches = [
        pltpu.make_async_copy(src, dst, fetched.at[i])
        for i, (src, dst) in enumerate((
            (gate_ref, w_ref.at[:, pl.ds(0, hidden)]),
            (up_ref, w_ref.at[:, pl.ds(hidden, hidden)]),
            (sent_hbm, sent_ref),
            (got_hbm, got_ref),
            (cot_hbm, cot_ref),
        ))
    ]
    for fetch in fetches:
        fetch.start()
    greet(index)
    for fetch in fetches[:2]:
        fetch.wait()
    keep = pltpu.make_async_copy(w_ref, out_ref.at[pl.ds(pl.multiple_of(index(0, 0) * rows, rows), rows), :], own)
    keep.start()
    for part in (0, 1):
        y_copy("b", 0, 0, part, True).start()
    for way in (0, 1):
        z_copy("a", way, 1, True).start()
    for part in (0, 1):
        y_copy("a", 0, 0, part, True).start()
    for way in (0, 1):
        z_copy(0, way, 1, True).start()

    def move(stream, way, k, known):
        if known and k > reach(nz, stream, way):
            return False
        z_wait(stream, way, k)
        if not known or k + 1 <= reach(nz, stream, way):
            z_copy(stream, way, k + 1).start()
        return True

    def a_step(k, known):
        for way in (0, 1):
            if move("a", way, k, known):
                for part in (0, 1):
                    y_copy(sort(way), origin(way, k), cell(way, k), part).start()

    def a_pass(k, known):
        for way in (0, 1):
            if not known or k <= reach(nz, "a", way):
                y_pass(sort(way), origin(way, k), cell(way, k))

    def b_step(k, known):
        for stream in (0, 3, 1, 2):
            for way in (0, 1):
                move(stream, way, k, known)

    for fetch in fetches[2:]:
        fetch.wait()
    change = jnp.sum((sent_ref[...] - got_ref[...]).astype(jnp.float32), axis=1, keepdims=True)
    row = lax.broadcasted_iota(jnp.int32, (cot_ref.shape[0], 128), 0).astype(jnp.float32)
    live = row < jnp.broadcast_to(change + BAL, row.shape)
    for start in range(0, cot_ref.shape[1], 128):
        value = cot_ref[:, pl.ds(start, 128)].astype(jnp.float32)
        cot_live_ref[:, pl.ds(start, 128)] = jnp.where(live, value, 0.0).astype(cot_live_ref.dtype)

    a_step(1, True)
    for part in (0, 1):
        y_wait("b", 0, 0, part)
        y_copy("b", 0, 0, part + 2).start()
        for way in (0, 1):
            z_copy(3 if part == 0 else 1, way, 1).start()
    y_pass("a", 0, 0)
    a_step(2, top > 2 and 2 >= top - 1 or top == 2)
    for part in (2, 3):
        y_wait("b", 0, 0, part)
    for way in (0, 1):
        z_copy(2, way, 1).start()

    def body(k, carry):
        a_step(k, False)
        b_step(k - 2, False)
        a_pass(k - 2, False)
        return carry

    if top > 4:
        lax.fori_loop(3, top - 1, body, 0)
    for k in range(max(3, top - 1), top + 1):
        a_step(k, True)
        b_step(k - 2, True)
        a_pass(k - 2, True)
    a_pass(top - 1, True)
    b_step(top - 1, True)
    a_pass(top, True)
    b_step(top, True)

    def drain_y(kind, c, zo):
        for part in (2, 3):
            y_wait(kind, zo, c, part)
        for part in range(4):
            y_copy(kind, zo, c, part).wait_send()

    drain_y("a", 0, 0)
    for part in range(4):
        y_copy("b", 0, 0, part).wait_send()

    def drain(k, known):
        for way in (0, 1):
            for stream in ("a", 0, 1, 2, 3):
                if not known or k <= reach(nz, stream, way):
                    z_copy(stream, way, k).wait_send()
            if not known or k <= reach(nz, "a", way):
                drain_y(sort(way), cell(way, k), origin(way, k))

    def drain_body(k, carry):
        drain(k, False)
        return carry

    lax.fori_loop(1, top, drain_body, 0)
    drain(top, True)
    keep.wait()


def gather_rows(w_gate, w_up, sent, got, cotangent, ranks):
    rows, cols = w_gate.shape[0], 2 * w_gate.shape[1]
    nz = ranks // RING_Y
    tiles = cols // 128
    cut = 128 * max(2, round(tiles * 0.633))
    half_a = 128 * ((cut // 128 + 1) // 2)
    half_b = 128 * (((cols - cut) // 128 + 1) // 2)
    dma = pltpu.SemaphoreType.DMA
    k = nz // 2 + 1
    return pl.pallas_call(
        functools.partial(gather_kernel, nz, cut, half_a, half_b),
        out_shape=(
            jax.ShapeDtypeStruct((ranks * rows, cols), w_gate.dtype),
            jax.ShapeDtypeStruct(cotangent.shape, cotangent.dtype),
        ),
        in_specs=[HBM] * 5,
        out_specs=(VMEM, VMEM),
        scratch_shapes=[
            pltpu.VMEM((rows, cols), w_gate.dtype),
            pltpu.VMEM(sent.shape, sent.dtype),
            pltpu.VMEM(got.shape, got.dtype),
            pltpu.VMEM(cotangent.shape, cotangent.dtype),
            dma((5,)),
            dma((2, k)), dma((2, k)), dma((2, k, 4)), dma((2, k, 4)),
            dma((nz, 4)), dma((nz, 4)), dma((4,)), dma((4,)), dma,
        ],
        compiler_params=pltpu.CompilerParams(
            collective_id=0, has_side_effects=True, vmem_limit_bytes=20 * 1024 * 1024),
        name="gather_rows",
    )(*(pltpu.with_memory_space_constraint(a, pltpu.HBM) for a in (w_gate, w_up, sent, got, cotangent)))


def scatter_kernel(
    nz, peers, cut, half_a, half_b, p_ref, d_ref, weights_ref, out_ref, grad_x_ref, part_out, part_in,
    far, near, near_out, za_in, za_out, zb_in, zb_out, b_sum, b_far, b_near, b_near_out,
    part_s, part_r, far_s, far_r, near_s, near_r, za_s, za_r, zb_s, zb_r, bf_s, bf_r, bn_s, bn_r,
):
    index = place(nz)
    rows, cols = out_ref.shape
    top = nz // 2
    f32, bf16 = jnp.float32, jnp.bfloat16
    wide_b = cols - cut
    halves_a = ((0, half_a), (half_a, cut - half_a))
    halves_b = ((0, half_b), (half_b, wide_b - half_b))

    def mine(yo, zo, start, size):
        row = pl.multiple_of(index(yo, zo) * rows, rows)
        return p_ref.at[pl.ds(row, rows), pl.ds(start, size)]

    def copy(src, dst, target, s_sem, r_sem):
        return pltpu.make_async_remote_copy(
            src_ref=src, dst_ref=dst, send_sem=s_sem, recv_sem=r_sem,
            device_id={"dp": index(*target)}, device_id_type=MESH,
        )

    side = ((1, 0), (-1, 0))
    onward = ((0, 1), (0, -1))

    def toward(way, m):
        return m if way == 0 else -m

    def cell(way, m):
        return 2 * m - 1 + way

    def far_copy(zo, c, part):
        start, size = halves_a[part]
        return copy(mine(2, zo, start, size), far.at[c, :, pl.ds(start, size)], side[part],
                    far_s.at[c, part], far_r.at[c, part])

    def near_copy(c, part):
        return copy(near_out.at[c, part], near.at[c, part], side[part],
                    near_s.at[c, part], near_r.at[c, part])

    def stage_1(zo, c):
        for part in (0, 1):
            far_copy(zo, c, part).start()

    def stage_2(zo, c):
        for part in (0, 1):
            start, size = halves_a[part]
            rest, rest_size = halves_a[1 - part]
            yo = 1 if part == 0 else -1
            near_out[c, part, :, pl.ds(rest, rest_size)] = mine(yo, zo, rest, rest_size)[...]
            far_copy(zo, c, part).wait_recv()
            total = mine(yo, zo, start, size)[...].astype(f32) + far[c, :, pl.ds(start, size)].astype(f32)
            near_out[c, part, :, pl.ds(start, size)] = total.astype(bf16)
            near_copy(c, part).start()

    def stage_3(zo, c):
        for part in (0, 1):
            near_copy(c, part).wait_recv()
        return (mine(0, zo, 0, cut)[...].astype(f32) + near[c, 0].astype(f32)) + near[c, 1].astype(f32)

    def za_copy(way, m):
        return copy(za_out.at[way, m], za_in.at[way, m], onward[way], za_s.at[way, m], za_r.at[way, m])

    def zb_copy(way, m, stream, src=None):
        return copy(zb_out.at[way, m, stream] if src is None else src, zb_in.at[way, m, stream],
                    onward[way], zb_s.at[way, m, stream], zb_r.at[way, m, stream])

    def cells(m, known):
        if known and m == 0:
            return ((0, 0),)
        return tuple((toward(way, m), cell(way, m)) for way in (0, 1)
                     if not known or m <= reach(nz, "a", way))

    def ahead(m, known, stage):
        for zo, c in cells(m, known):
            stage(zo, c)

    def b_step(m, known):
        for stream in (0, 1, 2, 3):
            for way in (0, 1):
                limit = reach(nz, stream, way)
                if known and m > limit:
                    continue
                block = mine(stream, toward(way, m), cut, wide_b)
                if known and m == limit:
                    zb_copy(way, m - 1, stream, block).start()
                else:
                    zb_copy(way, m, stream).wait_recv()
                    total = block[...].astype(f32) + zb_in[way, m, stream].astype(f32)
                    zb_out[way, m - 1, stream] = total.astype(bf16)
                    zb_copy(way, m - 1, stream).start()

    def a_step(m, known):
        for way in (0, 1):
            limit = reach(nz, "a", way)
            if known and m > limit:
                continue
            total = stage_3(toward(way, m), cell(way, m))
            if not (known and m == limit):
                za_copy(way, m).wait_recv()
                total = total + za_in[way, m].astype(f32)
            za_out[way, m - 1] = total.astype(bf16)
            za_copy(way, m - 1).start()

    group = lax.axis_index("mp")
    width = grad_x_ref.shape[1]

    chips = peers // 2
    chip, core = lax.div(group, 2), lax.rem(group, 2)

    def owner(j, same):
        return lax.rem(chip + j, chips) * 2 + (core if same else 1 - core)

    def part_copy(i, target):
        return pltpu.make_async_remote_copy(
            src_ref=part_out.at[i], dst_ref=part_in.at[i], send_sem=part_s.at[i], recv_sem=part_r.at[i],
            device_id={"mp": target}, device_id_type=MESH,
        )

    def chip_copy(j):
        return part_copy(j, owner(j, True))

    def pair_copy(j):
        return part_copy(chips + j, owner(0, False))

    def share(i, target):
        row = pl.multiple_of(target * width, width)
        part_out[i] = lax.dot_general(
            d_ref[...], weights_ref[pl.ds(row, width), :], (((1,), (1,)), ((), ())),
            preferred_element_type=f32,
        ).astype(bf16)

    def pair_sum(j):
        pair_copy(j).wait_recv()
        return part_out[j].astype(f32) + part_in[chips + j].astype(f32)

    tour = sorted(range(chips), key=lambda j: -min(j, chips - j))
    jobs = [(j, same) for j in tour for same in (False, True)]
    ready = []

    def advance():
        if ready:
            j = ready.pop(0)
            part_out[j] = pair_sum(j).astype(bf16)
            chip_copy(j).start()
        if jobs:
            j, same = jobs.pop(0)
            share(j if same else chips + j, owner(j, same))
            if not same:
                pair_copy(j).start()
            elif j:
                ready.append(j)

    greet(index, [owner(0, False)] + [owner(j, True) for j in range(1, chips)])
    b_step(top, True)
    ahead(top, True, stage_1)
    ahead(top - 1, True, stage_1)
    ahead(top - 2, True, stage_1)
    advance()
    ahead(top, True, stage_2)
    b_step(top - 1, True)
    advance()
    ahead(top - 1, True, stage_2)
    ahead(top - 3, True, stage_1)

    def iterate(m, known):
        if not known or m >= 4:
            ahead(m - 4, known, stage_1)
        if not known or m >= 3:
            b_step(m - 2, known)
        if not known or m >= 2:
            ahead(m - 2, known, stage_2)
        a_step(m, known)
        advance()

    for m in range(top, 2, -1):
        iterate(m, True)

    def b_final(stream):
        total = mine(stream, 0, cut, wide_b)[...].astype(f32)
        for way in (0, 1):
            zb_copy(way, 0, stream).wait_recv()
            total = total + zb_in[way, 0, stream].astype(f32)
        return total

    def bf_copy(part):
        start, size = halves_b[part]
        return copy(b_sum.at[:, pl.ds(start, size)], b_far.at[:, pl.ds(start, size)], side[part],
                    bf_s.at[part], bf_r.at[part])

    def bn_copy(part):
        return copy(b_near_out.at[part], b_near.at[part], side[part], bn_s.at[part], bn_r.at[part])

    b_sum[...] = b_final(2).astype(bf16)
    for part in (0, 1):
        bf_copy(part).start()
    iterate(2, True)
    next_to = (b_final(1), b_final(3))
    own_b = b_final(0)
    for part in (0, 1):
        start, size = halves_b[part]
        rest, rest_size = halves_b[1 - part]
        bf_copy(part).wait_recv()
        total = next_to[part]
        b_near_out[part, :, pl.ds(rest, rest_size)] = total[:, rest:rest + rest_size].astype(bf16)
        b_near_out[part, :, pl.ds(start, size)] = (
            total[:, start:start + size] + b_far[:, pl.ds(start, size)].astype(f32)).astype(bf16)
        bn_copy(part).start()
    iterate(1, True)
    while jobs or ready:
        advance()
    grad_x = pair_sum(0)
    for j in range(1, chips):
        chip_copy(j).wait_recv()
        grad_x = grad_x + part_in[j].astype(f32)
    grad_x_ref[...] = grad_x.astype(bf16)
    total = stage_3(0, 0)
    for way in (0, 1):
        za_copy(way, 0).wait_recv()
        total = total + za_in[way, 0].astype(f32)
    out_ref[:, pl.ds(0, cut)] = total
    for part in (0, 1):
        bn_copy(part).wait_recv()
    out_ref[:, pl.ds(cut, wide_b)] = (own_b + b_near[0].astype(f32)) + b_near[1].astype(f32)

    def drain_y(zo, c):
        for part in (0, 1):
            far_copy(zo, c, part).wait_send()
            near_copy(c, part).wait_send()

    def drain(m, known):
        ahead(m, known, drain_y)
        for way in (0, 1):
            for stream in (0, 1, 2, 3):
                if not known or m <= reach(nz, stream, way):
                    zb_copy(way, m - 1, stream).wait_send()
            if not known or m <= reach(nz, "a", way):
                za_copy(way, m - 1).wait_send()

    drain_y(0, 0)

    def drain_body(m, carry):
        drain(m, False)
        return carry

    lax.fori_loop(1, top, drain_body, 0)
    drain(top, True)
    for part in (0, 1):
        bf_copy(part).wait_send()
        bn_copy(part).wait_send()
    for j in range(chips):
        pair_copy(j).wait_send()
        if j:
            chip_copy(j).wait_send()


def scatter_sum(whole, d_both, weights, ranks, peers):
    rows, cols = whole.shape[0] // ranks, whole.shape[1]
    nz = ranks // RING_Y
    tiles = cols // 128
    cut = 128 * max(2, round(tiles * 0.55))
    half_a = 128 * ((cut // 128 + 1) // 2)
    wide_b = cols - cut
    half_b = 128 * ((wide_b // 128 + 1) // 2)
    k = nz // 2 + 1
    tokens, width = d_both.shape[0], weights.shape[0] // peers
    bf16 = jnp.bfloat16
    dma = pltpu.SemaphoreType.DMA
    return pl.pallas_call(
        functools.partial(scatter_kernel, nz, peers, cut, half_a, half_b),
        out_shape=(
            jax.ShapeDtypeStruct((rows, cols), jnp.float32),
            jax.ShapeDtypeStruct((tokens, width), bf16),
        ),
        in_specs=[VMEM] * 3,
        out_specs=(VMEM, VMEM),
        scratch_shapes=[
            pltpu.VMEM((peers, tokens, width), bf16),
            pltpu.VMEM((peers, tokens, width), bf16),
            pltpu.VMEM((nz, rows, cut), bf16),
            pltpu.VMEM((nz, 2, rows, cut), bf16),
            pltpu.VMEM((nz, 2, rows, cut), bf16),
            pltpu.VMEM((2, k, rows, cut), bf16),
            pltpu.VMEM((2, k, rows, cut), bf16),
            pltpu.VMEM((2, k, 4, rows, wide_b), bf16),
            pltpu.VMEM((2, k, 4, rows, wide_b), bf16),
            pltpu.VMEM((rows, wide_b), bf16),
            pltpu.VMEM((rows, wide_b), bf16),
            pltpu.VMEM((2, rows, wide_b), bf16),
            pltpu.VMEM((2, rows, wide_b), bf16),
            dma((peers,)), dma((peers,)),
            dma((nz, 2)), dma((nz, 2)), dma((nz, 2)), dma((nz, 2)),
            dma((2, k)), dma((2, k)), dma((2, k, 4)), dma((2, k, 4)),
            dma((2,)), dma((2,)), dma((2,)), dma((2,)),
        ],
        compiler_params=pltpu.CompilerParams(
            collective_id=1, has_side_effects=True, vmem_limit_bytes=32 * 1024 * 1024),
        name="scatter_sum",
    )(whole, d_both, weights)


def on_device(x_in, cotangent, w_gate, w_up, send_counts, recv_counts):
    ranks = lax.axis_size("dp")
    hidden = w_gate.shape[1]
    weights, cot_live = gather_rows(w_gate, w_up, send_counts, recv_counts, cotangent, ranks)
    both = jnp.dot(x_in, weights, preferred_element_type=jnp.float32)
    gate_val, up_val = both[:, :hidden], both[:, hidden:]
    sig = jax.nn.sigmoid(gate_val)
    cot_val = cot_live.astype(jnp.float32)
    d_gate = (cot_val * up_val * sig * (1.0 + gate_val * (1.0 - sig))).astype(jnp.bfloat16)
    d_up = (cot_val * gate_val * sig).astype(jnp.bfloat16)
    whole = lax.dot_general(
        x_in, d_gate, (((0,), (0,)), ((), ())), preferred_element_type=jnp.float32
    ).astype(jnp.bfloat16)
    grad_gate, grad_x = scatter_sum(
        whole, jnp.concatenate([d_gate, d_up], axis=1), weights, ranks, lax.axis_size("mp"))
    return (grad_x, grad_gate)


def solution(mesh):
    return jax.shard_map(
        on_device,
        mesh=mesh,
        in_specs=(
            P("dp", None),
            P("dp", "mp"),
            P("dp", "mp"),
            P("dp", "mp"),
            P("dp", None),
            P("dp", None),
        ),
        out_specs=(P("dp", "mp"), P("dp", "mp")),
        check_vma=False,
    )
```

```python
import functools

import jax
import jax.numpy as jnp
from jax import lax
from jax.experimental import pallas as pl
from jax.experimental.pallas import tpu as pltpu
from jax.sharding import PartitionSpec as P

BAL = 208
RING_Y = 4
MESH = pl.DeviceIdType.MESH
VMEM = pl.BlockSpec(memory_space=pltpu.VMEM)
HBM = pl.BlockSpec(memory_space=pltpu.HBM)


def place(nz):
    me = lax.axis_index("dp")
    y, z = lax.div(me, nz), lax.rem(me, nz)

    def index(yo, zo):
        return lax.rem(y + yo + 2 * RING_Y, RING_Y) * nz + lax.rem(z + zo + 2 * nz, nz)

    return index


def greet(index, peers=()):
    barrier = pltpu.get_barrier_semaphore()
    for peer in peers:
        pl.semaphore_signal(barrier, inc=1, device_id={"mp": peer}, device_id_type=MESH)
    for yo, zo in ((0, 1), (0, -1), (1, 0), (-1, 0)):
        pl.semaphore_signal(
            barrier, inc=1, device_id={"dp": index(yo, zo)}, device_id_type=MESH
        )
    pl.semaphore_wait(barrier, 4 + len(peers))


def reach(nz, stream, way):
    forward = stream in ("a", 0)
    return nz // 2 if forward == (way == 0) else nz // 2 - 1


def gather_kernel(
    nz, cut, half_a, half_b, gate_ref, up_ref, sent_hbm, got_hbm, cot_hbm, out_ref, cot_live_ref,
    w_ref, sent_ref, got_ref, cot_ref, fetched,
    za_s, za_r, zb_s, zb_r, ya_s, ya_r, yb_s, yb_r, own
):
    index = place(nz)
    rows, cols = w_ref.shape
    top = nz // 2
    spans = {"a": (0, cut), "b": (cut, cols - cut)}
    halves = {
        "a": ((0, half_a), (half_a, cut - half_a)),
        "a_odd": ((half_a, cut - half_a), (0, half_a)),
        "b": ((cut, half_b), (cut + half_b, cols - cut - half_b)),
    }

    def block(yo, zo, span):
        start = pl.multiple_of(index(yo, zo) * rows, rows)
        return out_ref.at[pl.ds(start, rows), pl.ds(span[0], span[1])]

    def copy(src, dst, target, s_sem, r_sem):
        return pltpu.make_async_remote_copy(
            src_ref=src, dst_ref=dst, send_sem=s_sem, recv_sem=r_sem,
            device_id={"dp": index(*target)}, device_id_type=MESH,
        )

    def origin(way, k):
        return -k if way == 0 else k

    def onward(way):
        return (0, 1) if way == 0 else (0, -1)

    def z_copy(stream, way, k, mine=False):
        span = spans["a"] if stream == "a" else spans["b"]
        yo = 0 if stream == "a" else stream
        dst = block(yo, origin(way, k - 1), span)
        src = w_ref.at[:, pl.ds(span[0], span[1])] if mine else dst
        sems = (za_s.at[way, k], za_r.at[way, k]) if stream == "a" else (
            zb_s.at[way, k, stream], zb_r.at[way, k, stream])
        return copy(src, dst, onward(way), *sems)

    def z_wait(stream, way, k):
        span = spans["a"] if stream == "a" else spans["b"]
        yo = 0 if stream == "a" else stream
        dst = block(yo, origin(way, k), span)
        sem = za_r.at[way, k] if stream == "a" else zb_r.at[way, k, stream]
        other = za_s.at[way, k] if stream == "a" else zb_s.at[way, k, stream]
        copy(dst, dst, onward(way), other, sem).wait_recv()

    def y_sems(kind, c, part):
        if kind != "b":
            return ya_s.at[c, part], ya_r.at[c, part]
        return yb_s.at[part], yb_r.at[part]

    def y_part(kind, part):
        return spans[kind[0]] if part < 2 else halves[kind][part - 2]

    def y_copy(kind, zo, c, part, mine=False):
        span = y_part(kind, part)
        yo = 0 if part < 2 else (-1 if part == 2 else 1)
        dst = block(yo, zo, span)
        src = w_ref.at[:, pl.ds(span[0], span[1])] if mine else dst
        return copy(src, dst, (1, 0) if part % 2 == 0 else (-1, 0), *y_sems(kind, c, part))

    def y_wait(kind, zo, c, part):
        yo = (-1, 1, -2, 2)[part]
        dst = block(yo, zo, y_part(kind, part))
        copy(dst, dst, (1, 0), *y_sems(kind, c, part)).wait_recv()

    def cell(way, k):
        return 2 * k - 1 + way

    def sort(way):
        return ("a_odd", "a")[way]

    def y_pass(kind, zo, c):
        for part in (0, 1):
            y_wait(kind, zo, c, part)
            y_copy(kind, zo, c, part + 2).start()

    hidden = gate_ref.shape[1]
    fetches = [
        pltpu.make_async_copy(src, dst, fetched.at[i])
        for i, (src, dst) in enumerate((
            (gate_ref, w_ref.at[:, pl.ds(0, hidden)]),
            (up_ref, w_ref.at[:, pl.ds(hidden, hidden)]),
            (sent_hbm, sent_ref),
            (got_hbm, got_ref),
            (cot_hbm, cot_ref),
        ))
    ]
    for fetch in fetches:
        fetch.start()
    greet(index)
    for fetch in fetches[:2]:
        fetch.wait()
    keep = pltpu.make_async_copy(w_ref, out_ref.at[pl.ds(pl.multiple_of(index(0, 0) * rows, rows), rows), :], own)
    keep.start()
    for part in (0, 1):
        y_copy("b", 0, 0, part, True).start()
    for way in (0, 1):
        z_copy("a", way, 1, True).start()
    for part in (0, 1):
        y_copy("a", 0, 0, part, True).start()
    for way in (0, 1):
        z_copy(0, way, 1, True).start()

    def move(stream, way, k, known):
        if known and k > reach(nz, stream, way):
            return False
        z_wait(stream, way, k)
        if not known or k + 1 <= reach(nz, stream, way):
            z_copy(stream, way, k + 1).start()
        return True

    def a_step(k, known):
        for way in (0, 1):
            if move("a", way, k, known):
                for part in (0, 1):
                    y_copy(sort(way), origin(way, k), cell(way, k), part).start()

    def a_pass(k, known):
        for way in (0, 1):
            if not known or k <= reach(nz, "a", way):
                y_pass(sort(way), origin(way, k), cell(way, k))

    def b_step(k, known):
        for stream in (0, 3, 1, 2):
            for way in (0, 1):
                move(stream, way, k, known)

    for fetch in fetches[2:]:
        fetch.wait()
    change = jnp.sum((sent_ref[...] - got_ref[...]).astype(jnp.float32), axis=1, keepdims=True)
    row = lax.broadcasted_iota(jnp.int32, (cot_ref.shape[0], 128), 0).astype(jnp.float32)
    live = row < jnp.broadcast_to(change + BAL, row.shape)
    for start in range(0, cot_ref.shape[1], 128):
        value = cot_ref[:, pl.ds(start, 128)].astype(jnp.float32)
        cot_live_ref[:, pl.ds(start, 128)] = jnp.where(live, value, 0.0).astype(cot_live_ref.dtype)

    a_step(1, True)
    for part in (0, 1):
        y_wait("b", 0, 0, part)
        y_copy("b", 0, 0, part + 2).start()
        for way in (0, 1):
            z_copy(3 if part == 0 else 1, way, 1).start()
    y_pass("a", 0, 0)
    a_step(2, top > 2 and 2 >= top - 1 or top == 2)
    for part in (2, 3):
        y_wait("b", 0, 0, part)
    for way in (0, 1):
        z_copy(2, way, 1).start()

    def body(k, carry):
        a_step(k, False)
        b_step(k - 2, False)
        a_pass(k - 2, False)
        return carry

    if top > 4:
        lax.fori_loop(3, top - 1, body, 0)
    for k in range(max(3, top - 1), top + 1):
        a_step(k, True)
        b_step(k - 2, True)
        a_pass(k - 2, True)
    a_pass(top - 1, True)
    b_step(top - 1, True)
    a_pass(top, True)
    b_step(top, True)

    def drain_y(kind, c, zo):
        for part in (2, 3):
            y_wait(kind, zo, c, part)
        for part in range(4):
            y_copy(kind, zo, c, part).wait_send()

    drain_y("a", 0, 0)
    for part in range(4):
        y_copy("b", 0, 0, part).wait_send()

    def drain(k, known):
        for way in (0, 1):
            for stream in ("a", 0, 1, 2, 3):
                if not known or k <= reach(nz, stream, way):
                    z_copy(stream, way, k).wait_send()
            if not known or k <= reach(nz, "a", way):
                drain_y(sort(way), cell(way, k), origin(way, k))

    def drain_body(k, carry):
        drain(k, False)
        return carry

    lax.fori_loop(1, top, drain_body, 0)
    drain(top, True)
    keep.wait()


def gather_rows(w_gate, w_up, sent, got, cotangent, ranks):
    rows, cols = w_gate.shape[0], 2 * w_gate.shape[1]
    nz = ranks // RING_Y
    tiles = cols // 128
    cut = 128 * max(2, round(tiles * 0.633))
    half_a = 128 * ((cut // 128 + 1) // 2)
    half_b = 128 * (((cols - cut) // 128 + 1) // 2)
    dma = pltpu.SemaphoreType.DMA
    k = nz // 2 + 1
    return pl.pallas_call(
        functools.partial(gather_kernel, nz, cut, half_a, half_b),
        out_shape=(
            jax.ShapeDtypeStruct((ranks * rows, cols), w_gate.dtype),
            jax.ShapeDtypeStruct(cotangent.shape, cotangent.dtype),
        ),
        in_specs=[HBM] * 5,
        out_specs=(VMEM, VMEM),
        scratch_shapes=[
            pltpu.VMEM((rows, cols), w_gate.dtype),
            pltpu.VMEM(sent.shape, sent.dtype),
            pltpu.VMEM(got.shape, got.dtype),
            pltpu.VMEM(cotangent.shape, cotangent.dtype),
            dma((5,)),
            dma((2, k)), dma((2, k)), dma((2, k, 4)), dma((2, k, 4)),
            dma((nz, 4)), dma((nz, 4)), dma((4,)), dma((4,)), dma,
        ],
        compiler_params=pltpu.CompilerParams(
            collective_id=0, has_side_effects=True, vmem_limit_bytes=20 * 1024 * 1024),
        name="gather_rows",
    )(*(pltpu.with_memory_space_constraint(a, pltpu.HBM) for a in (w_gate, w_up, sent, got, cotangent)))


def scatter_kernel(
    nz, peers, cut, half_a, half_b, p_ref, d_ref, weights_ref, out_ref, grad_x_ref, part_out, part_in,
    far, near, near_out, za_in, za_out, zb_in, zb_out, b_sum, b_far, b_near, b_near_out,
    part_s, part_r, far_s, far_r, near_s, near_r, za_s, za_r, zb_s, zb_r, bf_s, bf_r, bn_s, bn_r,
):
    index = place(nz)
    rows, cols = out_ref.shape
    top = nz // 2
    f32, bf16 = jnp.float32, jnp.bfloat16
    wide_b = cols - cut
    halves_a = ((0, half_a), (half_a, cut - half_a))
    halves_b = ((0, half_b), (half_b, wide_b - half_b))

    def mine(yo, zo, start, size):
        row = pl.multiple_of(index(yo, zo) * rows, rows)
        return p_ref.at[pl.ds(row, rows), pl.ds(start, size)]

    def copy(src, dst, target, s_sem, r_sem):
        return pltpu.make_async_remote_copy(
            src_ref=src, dst_ref=dst, send_sem=s_sem, recv_sem=r_sem,
            device_id={"dp": index(*target)}, device_id_type=MESH,
        )

    side = ((1, 0), (-1, 0))
    onward = ((0, 1), (0, -1))

    def toward(way, m):
        return m if way == 0 else -m

    def cell(way, m):
        return 2 * m - 1 + way

    def far_copy(zo, c, part):
        start, size = halves_a[part]
        return copy(mine(2, zo, start, size), far.at[c, :, pl.ds(start, size)], side[part],
                    far_s.at[c, part], far_r.at[c, part])

    def near_copy(c, part):
        return copy(near_out.at[c, part], near.at[c, part], side[part],
                    near_s.at[c, part], near_r.at[c, part])

    def stage_1(zo, c):
        for part in (0, 1):
            far_copy(zo, c, part).start()

    def stage_2(zo, c):
        for part in (0, 1):
            start, size = halves_a[part]
            rest, rest_size = halves_a[1 - part]
            yo = 1 if part == 0 else -1
            near_out[c, part, :, pl.ds(rest, rest_size)] = mine(yo, zo, rest, rest_size)[...]
            far_copy(zo, c, part).wait_recv()
            total = mine(yo, zo, start, size)[...].astype(f32) + far[c, :, pl.ds(start, size)].astype(f32)
            near_out[c, part, :, pl.ds(start, size)] = total.astype(bf16)
            near_copy(c, part).start()

    def stage_3(zo, c):
        for part in (0, 1):
            near_copy(c, part).wait_recv()
        return (mine(0, zo, 0, cut)[...].astype(f32) + near[c, 0].astype(f32)) + near[c, 1].astype(f32)

    def za_copy(way, m):
        return copy(za_out.at[way, m], za_in.at[way, m], onward[way], za_s.at[way, m], za_r.at[way, m])

    def zb_copy(way, m, stream, src=None):
        return copy(zb_out.at[way, m, stream] if src is None else src, zb_in.at[way, m, stream],
                    onward[way], zb_s.at[way, m, stream], zb_r.at[way, m, stream])

    def cells(m, known):
        if known and m == 0:
            return ((0, 0),)
        return tuple((toward(way, m), cell(way, m)) for way in (0, 1)
                     if not known or m <= reach(nz, "a", way))

    def ahead(m, known, stage):
        for zo, c in cells(m, known):
            stage(zo, c)

    def b_step(m, known):
        for stream in (0, 1, 2, 3):
            for way in (0, 1):
                limit = reach(nz, stream, way)
                if known and m > limit:
                    continue
                block = mine(stream, toward(way, m), cut, wide_b)
                if known and m == limit:
                    zb_copy(way, m - 1, stream, block).start()
                else:
                    zb_copy(way, m, stream).wait_recv()
                    total = block[...].astype(f32) + zb_in[way, m, stream].astype(f32)
                    zb_out[way, m - 1, stream] = total.astype(bf16)
                    zb_copy(way, m - 1, stream).start()

    def a_step(m, known):
        for way in (0, 1):
            limit = reach(nz, "a", way)
            if known and m > limit:
                continue
            total = stage_3(toward(way, m), cell(way, m))
            if not (known and m == limit):
                za_copy(way, m).wait_recv()
                total = total + za_in[way, m].astype(f32)
            za_out[way, m - 1] = total.astype(bf16)
            za_copy(way, m - 1).start()

    group = lax.axis_index("mp")
    width = grad_x_ref.shape[1]

    chips = peers // 2
    chip, core = lax.div(group, 2), lax.rem(group, 2)

    def owner(j, same):
        return lax.rem(chip + j, chips) * 2 + (core if same else 1 - core)

    def part_copy(i, target):
        return pltpu.make_async_remote_copy(
            src_ref=part_out.at[i], dst_ref=part_in.at[i], send_sem=part_s.at[i], recv_sem=part_r.at[i],
            device_id={"mp": target}, device_id_type=MESH,
        )

    def chip_copy(j):
        return part_copy(j, owner(j, True))

    def pair_copy(j):
        return part_copy(chips + j, owner(0, False))

    def share(i, target):
        row = pl.multiple_of(target * width, width)
        part_out[i] = lax.dot_general(
            d_ref[...], weights_ref[pl.ds(row, width), :], (((1,), (1,)), ((), ())),
            preferred_element_type=f32,
        ).astype(bf16)

    def pair_sum(j):
        pair_copy(j).wait_recv()
        return part_out[j].astype(f32) + part_in[chips + j].astype(f32)

    tour = sorted(range(chips), key=lambda j: -min(j, chips - j))
    jobs = [(j, same) for j in tour for same in (False, True)]
    ready = []

    def advance():
        if ready:
            j = ready.pop(0)
            part_out[j] = pair_sum(j).astype(bf16)
            chip_copy(j).start()
        if jobs:
            j, same = jobs.pop(0)
            share(j if same else chips + j, owner(j, same))
            if not same:
                pair_copy(j).start()
            elif j:
                ready.append(j)

    greet(index, [owner(0, False)] + [owner(j, True) for j in range(1, chips)])
    b_step(top, True)
    ahead(top, True, stage_1)
    ahead(top - 1, True, stage_1)
    ahead(top - 2, True, stage_1)
    advance()
    ahead(top, True, stage_2)
    b_step(top - 1, True)
    advance()
    ahead(top - 1, True, stage_2)
    ahead(top - 3, True, stage_1)

    def iterate(m, known):
        if not known or m >= 4:
            ahead(m - 4, known, stage_1)
        a_step(m, known)
        if not known or m >= 3:
            b_step(m - 2, known)
        if not known or m >= 2:
            ahead(m - 2, known, stage_2)
        advance()

    for m in range(top, 2, -1):
        iterate(m, True)

    def b_final(stream):
        total = mine(stream, 0, cut, wide_b)[...].astype(f32)
        for way in (0, 1):
            zb_copy(way, 0, stream).wait_recv()
            total = total + zb_in[way, 0, stream].astype(f32)
        return total

    def bf_copy(part):
        start, size = halves_b[part]
        return copy(b_sum.at[:, pl.ds(start, size)], b_far.at[:, pl.ds(start, size)], side[part],
                    bf_s.at[part], bf_r.at[part])

    def bn_copy(part):
        return copy(b_near_out.at[part], b_near.at[part], side[part], bn_s.at[part], bn_r.at[part])

    b_sum[...] = b_final(2).astype(bf16)
    for part in (0, 1):
        bf_copy(part).start()
    iterate(2, True)
    next_to = (b_final(1), b_final(3))
    own_b = b_final(0)
    for part in (0, 1):
        start, size = halves_b[part]
        rest, rest_size = halves_b[1 - part]
        bf_copy(part).wait_recv()
        total = next_to[part]
        b_near_out[part, :, pl.ds(rest, rest_size)] = total[:, rest:rest + rest_size].astype(bf16)
        b_near_out[part, :, pl.ds(start, size)] = (
            total[:, start:start + size] + b_far[:, pl.ds(start, size)].astype(f32)).astype(bf16)
        bn_copy(part).start()
    iterate(1, True)
    while jobs or ready:
        advance()
    grad_x = pair_sum(0)
    for j in range(1, chips):
        chip_copy(j).wait_recv()
        grad_x = grad_x + part_in[j].astype(f32)
    grad_x_ref[...] = grad_x.astype(bf16)
    total = stage_3(0, 0)
    for way in (0, 1):
        za_copy(way, 0).wait_recv()
        total = total + za_in[way, 0].astype(f32)
    out_ref[:, pl.ds(0, cut)] = total
    for part in (0, 1):
        bn_copy(part).wait_recv()
    out_ref[:, pl.ds(cut, wide_b)] = (own_b + b_near[0].astype(f32)) + b_near[1].astype(f32)

    def drain_y(zo, c):
        for part in (0, 1):
            far_copy(zo, c, part).wait_send()
            near_copy(c, part).wait_send()

    def drain(m, known):
        ahead(m, known, drain_y)
        for way in (0, 1):
            for stream in (0, 1, 2, 3):
                if not known or m <= reach(nz, stream, way):
                    zb_copy(way, m - 1, stream).wait_send()
            if not known or m <= reach(nz, "a", way):
                za_copy(way, m - 1).wait_send()

    drain_y(0, 0)

    def drain_body(m, carry):
        drain(m, False)
        return carry

    lax.fori_loop(1, top, drain_body, 0)
    drain(top, True)
    for part in (0, 1):
        bf_copy(part).wait_send()
        bn_copy(part).wait_send()
    for j in range(chips):
        pair_copy(j).wait_send()
        if j:
            chip_copy(j).wait_send()


def scatter_sum(whole, d_both, weights, ranks, peers):
    rows, cols = whole.shape[0] // ranks, whole.shape[1]
    nz = ranks // RING_Y
    tiles = cols // 128
    cut = 128 * max(2, round(tiles * 0.55))
    half_a = 128 * ((cut // 128 + 1) // 2)
    wide_b = cols - cut
    half_b = 128 * ((wide_b // 128 + 1) // 2)
    k = nz // 2 + 1
    tokens, width = d_both.shape[0], weights.shape[0] // peers
    bf16 = jnp.bfloat16
    dma = pltpu.SemaphoreType.DMA
    return pl.pallas_call(
        functools.partial(scatter_kernel, nz, peers, cut, half_a, half_b),
        out_shape=(
            jax.ShapeDtypeStruct((rows, cols), jnp.float32),
            jax.ShapeDtypeStruct((tokens, width), bf16),
        ),
        in_specs=[VMEM] * 3,
        out_specs=(VMEM, VMEM),
        scratch_shapes=[
            pltpu.VMEM((peers, tokens, width), bf16),
            pltpu.VMEM((peers, tokens, width), bf16),
            pltpu.VMEM((nz, rows, cut), bf16),
            pltpu.VMEM((nz, 2, rows, cut), bf16),
            pltpu.VMEM((nz, 2, rows, cut), bf16),
            pltpu.VMEM((2, k, rows, cut), bf16),
            pltpu.VMEM((2, k, rows, cut), bf16),
            pltpu.VMEM((2, k, 4, rows, wide_b), bf16),
            pltpu.VMEM((2, k, 4, rows, wide_b), bf16),
            pltpu.VMEM((rows, wide_b), bf16),
            pltpu.VMEM((rows, wide_b), bf16),
            pltpu.VMEM((2, rows, wide_b), bf16),
            pltpu.VMEM((2, rows, wide_b), bf16),
            dma((peers,)), dma((peers,)),
            dma((nz, 2)), dma((nz, 2)), dma((nz, 2)), dma((nz, 2)),
            dma((2, k)), dma((2, k)), dma((2, k, 4)), dma((2, k, 4)),
            dma((2,)), dma((2,)), dma((2,)), dma((2,)),
        ],
        compiler_params=pltpu.CompilerParams(
            collective_id=1, has_side_effects=True, vmem_limit_bytes=32 * 1024 * 1024),
        name="scatter_sum",
    )(whole, d_both, weights)


def on_device(x_in, cotangent, w_gate, w_up, send_counts, recv_counts):
    ranks = lax.axis_size("dp")
    hidden = w_gate.shape[1]
    weights, cot_live = gather_rows(w_gate, w_up, send_counts, recv_counts, cotangent, ranks)
    both = jnp.dot(x_in, weights, preferred_element_type=jnp.float32)
    gate_val, up_val = both[:, :hidden], both[:, hidden:]
    sig = jax.nn.sigmoid(gate_val)
    cot_val = cot_live.astype(jnp.float32)
    d_gate = (cot_val * up_val * sig * (1.0 + gate_val * (1.0 - sig))).astype(jnp.bfloat16)
    d_up = (cot_val * gate_val * sig).astype(jnp.bfloat16)
    whole = lax.dot_general(
        x_in, d_gate, (((0,), (0,)), ((), ())), preferred_element_type=jnp.float32
    ).astype(jnp.bfloat16)
    grad_gate, grad_x = scatter_sum(
        whole, jnp.concatenate([d_gate, d_up], axis=1), weights, ranks, lax.axis_size("mp"))
    return (grad_x, grad_gate)


def solution(mesh):
    return jax.shard_map(
        on_device,
        mesh=mesh,
        in_specs=(
            P("dp", None),
            P("dp", "mp"),
            P("dp", "mp"),
            P("dp", "mp"),
            P("dp", None),
            P("dp", None),
        ),
        out_specs=(P("dp", "mp"), P("dp", "mp")),
        check_vma=False,
    )
```
